32 devices in a mesh: seq: 8 (over z, x), batch: 4 (over y, core).
Axes of the slice: x: 2, y: 2, z: 4, core: 2. Of those that a mesh axis runs over, the one named last changes fastest.
Arguments:
- inputs: bfloat16 [32768, 768], P(('batch', 'seq')), parts along dimension 0, may hold values from -6 to 6
- token_rates: float32 [32768], P(('batch', 'seq')), parts along dimension 0, may hold values from 0.1 to 1
- proj_query: bfloat16 [768, 256], replicated, may hold values from -0.21875 to 0.21875
- proj_key: bfloat16 [768, 256], replicated, may hold values from -0.21875 to 0.21875
- proj_value: bfloat16 [768, 256], replicated, may hold values from -0.21875 to 0.21875
- proj_output: bfloat16 [256, 768], replicated, may hold values from -0.375 to 0.375
- fast_in: float32 [256, 512], replicated, may hold values from -0.375 to 0.375
- fast_up: float32 [256, 512], replicated, may hold values from -0.375 to 0.375
- fast_out: float32 [512, 256], replicated, may hold values from -0.25 to 0.25
- cotangent: bfloat16 [32768, 768], P(('batch', 'seq')), parts along dimension 0, may hold values from -6 to 6
Outputs:
- back_inputs: bfloat16 [32768, 768], P(('batch', 'seq')), parts along dimension 0
- back_rate: float32 [32768], P(('batch', 'seq')), parts along dimension 0
- grad_in: float32 [1024, 512], P('batch'), parts along dimension 0
- grad_up: float32 [1024, 512], P('batch'), parts along dimension 0
- grad_out: float32 [2048, 256], P('batch'), parts along dimension 0
- grad_query: float32 [768, 1024], P('seq', 'batch'), parts along dimension 1
- grad_key: float32 [768, 1024], P('seq', 'batch'), parts along dimension 1
- grad_value: float32 [768, 1024], P('seq', 'batch'), parts along dimension 1
- grad_output: float32 [1024, 768], P('batch', 'seq'), parts along dimension 0
The draws below stay inside these ranges and needn't reach their ends.
There are 4 independent parts, one for each index of `batch`. The reference program is written for one: setup_inputs(seed, part) draws one part's arguments, and reference() takes and returns one part's arrays. A program takes and returns all parts, laid end to end along the dimension named above; an argument that names none is the same for every part. Nothing has to cross between parts.
All inputs are finite; a program needn't handle non-finite values.
Results may differ from the reference program's by a relative error of at most 0.029.
Values may be sent and summed in bfloat16 or wider, within the bound.
A program may use at most 128 MiB of HBM per device.

```python
import math
import jax
import jax.numpy as jnp
from jax import lax

D = 768
H = 256
F = 512
NS_STEPS = 5
TOKENS = 8192


def raised(array, key, source, target, parts, factor):
    owner, partner = [(jnp.arange(array.shape[axis_at]) // (array.shape[axis_at] // parts)).reshape([-1 if axis == axis_at else 1 for axis in range(array.ndim)]) for axis_at in (source, target)]
    chosen = jax.random.permutation(key, parts)[partner]
    strong = (owner == chosen) | (owner == (partner + parts // 2) % parts)
    return jnp.where(strong, factor * array, array)


def shard_levels(stream_key, shape, split, low, largest):
    gain = 1.0
    for position, parts in split:
        steps = jax.random.uniform(jax.random.fold_in(jax.random.fold_in(stream_key, 6), position), (parts,), jnp.float32, low / len(split), largest / len(split))
        gain = gain * jnp.repeat(jnp.exp(steps), shape[position] // parts).reshape((-1,) + (1,) * (len(shape) - 1 - position))
    return gain


def gaussian(stream_key, dims, width, limit, cuts=(), held_as=jnp.bfloat16):
    array = width * jax.random.normal(stream_key, dims, jnp.float32)
    if cuts:
        array = array * shard_levels(stream_key, dims, cuts, -0.22, 0.18)
    return jnp.clip(array, -limit, limit).astype(held_as)


def bell_draw_with(key, extent, scale, limit, cuts, heavy, kind=jnp.bfloat16):
    drawn = scale * jax.random.normal(key, extent, jnp.float32)
    if cuts:
        drawn = drawn * shard_levels(key, extent, cuts, -0.22, 0.18)
    return jnp.clip(raised(drawn, jax.random.fold_in(key, 3), *heavy), -limit, limit).astype(kind)


def setup_inputs(seed: int = 0, part: int = 0) -> dict:
    key_list = jax.random.split(jax.random.key(seed), 11)
    part_keys = jax.random.split(jax.random.fold_in(key_list[10], part), 11)
    return {
        "inputs": bell_draw_with(part_keys[0], (TOKENS, D), 1.0, 6.0, ((0, 8),), (0, 1, 8, 2.0)),
        "token_rates": jnp.clip(jnp.exp(math.log(1.0) - 2.3025851 * jax.random.uniform(part_keys[1], (TOKENS,), jnp.float32) ** shard_levels(part_keys[1], (TOKENS,), ((0, 8),), -0.2, 0.2)), 0.1, 1.0),
        "proj_query": gaussian(key_list[2], (D, H), D ** -0.5, 0.21875),
        "proj_key": gaussian(key_list[3], (D, H), D ** -0.5, 0.21875),
        "proj_value": gaussian(key_list[4], (D, H), D ** -0.5, 0.21875),
        "proj_output": gaussian(key_list[5], (H, D), H ** -0.5, 0.375),
        "fast_in": gaussian(key_list[6], (H, F), H ** -0.5, 0.375, (), jnp.float32),
        "fast_up": gaussian(key_list[7], (H, F), H ** -0.5, 0.375, (), jnp.float32),
        "fast_out": gaussian(key_list[8], (F, H), F ** -0.5, 0.25, (), jnp.float32),
        "cotangent": bell_draw_with(part_keys[9], (TOKENS, D), 1.0, 6.0, ((0, 8),), (0, 1, 8, 2.0)),
    }


def rounded(value):
    return value.astype(jnp.bfloat16)

def product(left, right):
    return jnp.dot(left, right, preferred_element_type=jnp.float32)

def token_sum(left, right):
    return lax.dot_general(left, right, (((0,), (0,)), ((), ())), preferred_element_type=jnp.float32)

def times_transpose(left, right):
    return lax.dot_general(left, right, (((1,), (1,)), ((), ())), preferred_element_type=jnp.float32)

def silu_parts(pre_act):
    sigma_val = jax.nn.sigmoid(pre_act)
    activation = pre_act * sigma_val
    slope_val = sigma_val * (1.0 + pre_act * (1.0 - sigma_val))
    curvature = sigma_val * (1.0 - sigma_val) * (2.0 + pre_act * (1.0 - 2.0 * sigma_val))
    return (activation, slope_val, curvature)

def orthogonalize(matrix):
    highest = lax.Precision.HIGHEST
    current = matrix / (jnp.sqrt(jnp.sum(matrix * matrix)) + 1e-07)
    for sweep in range(NS_STEPS):
        gramian = jnp.dot(current, current.T, precision=highest)
        polynom = -4.775 * gramian + 2.0315 * jnp.dot(gramian, gramian, precision=highest)
        current = 3.4445 * current + jnp.dot(polynom, current, precision=highest)
    return current

def project(inputs, proj_query, proj_key, proj_value):
    return (rounded(product(inputs, proj_query)), rounded(product(inputs, proj_key)), rounded(product(inputs, proj_value)))

def update_section(key_rows, value_rows, token_rates, fast_in, fast_up, fast_out):
    w_in, w_up, w_out = (rounded(fast_in), rounded(fast_up), rounded(fast_out))
    scaled = rounded(token_rates[:, None] * value_rows.astype(jnp.float32))
    pre_in = product(key_rows, w_in)
    pre_up = product(key_rows, w_up)
    activation, slope_val, curvature = silu_parts(pre_in)
    hidden = rounded(activation * pre_up)
    upstream = times_transpose(scaled, w_out)
    grad_in_rows = rounded(upstream * pre_up * slope_val)
    grad_up_rows = rounded(upstream * activation)
    partial_value = jnp.stack([token_sum(key_rows, grad_in_rows), token_sum(key_rows, grad_up_rows), token_sum(scaled, hidden)])
    saved = (w_in, w_up, w_out, scaled, pre_in, pre_up, hidden, upstream, grad_in_rows, grad_up_rows)
    return (partial_value, saved)

def query_section(query_rows, cotangent, proj_output, new_in, new_up, new_out):
    n_in, n_up, n_out = (rounded(new_in), rounded(new_up), rounded(new_out))
    pre_p = product(query_rows, n_in)
    pre_r = product(query_rows, n_up)
    activation_q, slope_q, unused_curve = silu_parts(pre_p)
    hidden_q = rounded(activation_q * pre_r)
    output_rows = rounded(product(hidden_q, n_out))
    back_output = rounded(times_transpose(cotangent, proj_output))
    back_hidden = times_transpose(back_output, n_out)
    back_p = rounded(back_hidden * pre_r * slope_q)
    back_r = rounded(back_hidden * activation_q)
    partial_value = jnp.stack([token_sum(query_rows, back_p), token_sum(query_rows, back_r), token_sum(back_output, hidden_q)])
    query_grad = rounded(times_transpose(back_p, n_in) + times_transpose(back_r, n_up))
    return (partial_value, query_grad, output_rows)

def update_backward(saved, key_rows, value_rows, token_rates, back_totals):
    w_in, w_up, w_out, scaled, pre_in, pre_up, hidden, upstream, grad_in_rows, grad_up_rows = saved
    activation, slope_val, curvature = silu_parts(pre_in)
    b_in = rounded(back_totals[0])
    b_up = rounded(back_totals[1])
    b_out = rounded(back_totals[2])
    press_in = product(key_rows, b_in)
    press_up = product(key_rows, b_up)
    back_hid = product(scaled, b_out)
    back_upstream = rounded(press_in * pre_up * slope_val + press_up * activation)
    back_pre_up = rounded(press_in * upstream * slope_val + back_hid * activation)
    back_pre_in = rounded(press_in * upstream * pre_up * curvature + press_up * upstream * slope_val + back_hid * pre_up * slope_val)
    back_scaled = times_transpose(hidden, b_out) + product(back_upstream, w_out)
    back_rate = lax.optimization_barrier(jnp.sum(back_scaled * value_rows.astype(jnp.float32), axis=1))
    contrib = (token_sum(key_rows, back_pre_in), token_sum(key_rows, back_pre_up), token_sum(back_upstream, scaled))
    key_sum = times_transpose(grad_in_rows, b_in) + times_transpose(grad_up_rows, b_up)
    key_sum = key_sum + times_transpose(back_pre_in, w_in) + times_transpose(back_pre_up, w_up)
    key_grad = rounded(key_sum)
    value_grad = rounded(token_rates[:, None] * back_scaled)
    return (contrib, key_grad, value_grad, back_rate)

def input_back(query_grad, key_grad, value_grad, proj_query, proj_key, proj_value):
    total = times_transpose(query_grad, proj_query) + times_transpose(key_grad, proj_key)
    return rounded(total + times_transpose(value_grad, proj_value))

def reference(inputs, token_rates, proj_query, proj_key, proj_value, proj_output, fast_in, fast_up, fast_out, cotangent):
    query_rows, key_rows, value_rows = project(inputs, proj_query, proj_key, proj_value)
    totals, saved = update_section(key_rows, value_rows, token_rates, fast_in, fast_up, fast_out)
    ortho, ns_back = jax.vjp(jax.vmap(orthogonalize), totals)
    new_in = fast_in + ortho[0]
    new_up = fast_up + ortho[1]
    new_out = fast_out + ortho[2].T
    adjoint, query_grad, output_rows = query_section(query_rows, cotangent, proj_output, new_in, new_up, new_out)
    back_totals = ns_back(adjoint)[0]
    contrib, key_grad, value_grad, back_rate = update_backward(saved, key_rows, value_rows, token_rates, back_totals)
    grad_in = adjoint[0] + contrib[0]
    grad_up = adjoint[1] + contrib[1]
    grad_out = adjoint[2].T + contrib[2]
    back_inputs = input_back(query_grad, key_grad, value_grad, proj_query, proj_key, proj_value)
    grad_query = token_sum(inputs, query_grad)
    grad_key = token_sum(inputs, key_grad)
    grad_value = token_sum(inputs, value_grad)
    grad_output = token_sum(output_rows, cotangent)
    return (back_inputs, back_rate, grad_in, grad_up, grad_out, grad_query, grad_key, grad_value, grad_output)
```

```python
import functools
import math
from types import SimpleNamespace

import jax
import jax.numpy as jnp
from jax import lax
from jax.experimental import pallas as pl
from jax.experimental.pallas import tpu as pltpu
from jax.sharding import PartitionSpec as P

NS_STEPS = 5
NS_SINGLE = 2
C1, C3, C5 = 3.4445, -4.775, 2.0315
EPS = 1e-07
MESH = pl.DeviceIdType.MESH
VMEM_LIMIT = 66_000_000
PAIR = 2
COUNT = 3
LANES = 128
ROUNDS = 3
GROUPS = 4


def rounded(value):
    return value.astype(jnp.bfloat16)


def product(left, right):
    return jnp.dot(left, right, preferred_element_type=jnp.float32)


def token_sum(left, right):
    return lax.dot_general(
        left, right, (((0,), (0,)), ((), ())), preferred_element_type=jnp.float32
    )


def times_transpose(left, right):
    return lax.dot_general(
        left, right, (((1,), (1,)), ((), ())), preferred_element_type=jnp.float32
    )


def sigmoid_slope(pre_act):
    sigma = jax.nn.sigmoid(pre_act)
    return sigma, pre_act * sigma, sigma * (1.0 + pre_act * (1.0 - sigma))


def split(value):
    high = rounded(value)
    return (high, rounded(value - high.astype(jnp.float32)))


def dot_split(left, right, dot):
    along = 1 if dot is times_transpose else 0
    return dot(
        jnp.concatenate([left[0], left[0], left[1]], axis=1),
        jnp.concatenate([right[0], right[1], right[0]], axis=along),
    )


def place():
    me = lax.axis_index("seq")
    return me // PAIR, me % PAIR


def remote(src, dst, send, recv, device):
    copy = pltpu.make_async_remote_copy(
        src_ref=src,
        dst_ref=dst,
        send_sem=send,
        recv_sem=recv,
        device_id={"seq": device},
        device_id_type=MESH,
    )
    copy.start()
    return copy


def line_peer(lines, d):
    line, side = place()
    return lax.rem(line + d, lines) * PAIR + side


def partner():
    line, side = place()
    return line * PAIR + (1 - side)


def greet(lines):
    barrier = pltpu.get_barrier_semaphore()
    for peer in [partner()] + [line_peer(lines, d) for d in range(1, lines)]:
        pl.semaphore_signal(barrier, inc=1, device_id={"seq": peer}, device_id_type=MESH)


def greeted(lines):
    pl.semaphore_wait(pltpu.get_barrier_semaphore(), lines)


class Scatter:
    def __init__(self, lines, part, paired, middle, lined, sems):
        self.lines = lines
        self.part, self.paired, self.middle, self.lined = part, paired, middle, lined
        self.sems = sems

    def fill(self, total, at=0):
        n, rows, wide = self.part.shape
        for j in range(n):
            self.part[j] = rounded(total[j * rows : (j + 1) * rows, at : at + wide])

    def start(self):
        lines = self.lines
        line, side = place()
        self.pairs = {}
        for d in list(range(1, lines)) + [0]:
            to = lax.rem(line + d, lines)
            self.pairs[d] = remote(
                self.part.at[to * PAIR + (1 - side)],
                self.paired.at[d],
                self.sems.at[0, d],
                self.sems.at[1, d],
                partner(),
            )

    def forward(self):
        lines = self.lines
        line, side = place()
        self.sent = []
        for d in range(1, lines):
            to = lax.rem(line + d, lines)
            self.pairs[d].wait()
            self.middle[d] = rounded(
                self.part[to * PAIR + side].astype(jnp.float32)
                + self.paired[d].astype(jnp.float32)
            )
            self.sent.append(
                remote(
                    self.middle.at[d],
                    self.lined.at[d],
                    self.sems.at[2, d],
                    self.sems.at[3, d],
                    to * PAIR + side,
                )
            )

    def total(self):
        self.pairs[0].wait()
        me = lax.axis_index("seq")
        total = self.part[me].astype(jnp.float32) + self.paired[0].astype(jnp.float32)
        for d, copy in zip(range(1, self.lines), self.sent):
            copy.wait()
            total = total + self.lined[d].astype(jnp.float32)
        return total


class Reduce(Scatter):
    def __init__(self, lines, part, paired, middle, lined, sems, mine, gathered, crossed):
        super().__init__(lines, part, paired, middle, lined, sems)
        self.mine, self.gathered, self.crossed = mine, gathered, crossed

    def gather(self):
        self.mine[...] = rounded(self.total())
        self.out = []
        for d in range(1, self.lines):
            self.out.append(
                remote(
                    self.mine,
                    self.gathered.at[d],
                    self.sems.at[4, d],
                    self.sems.at[5, d],
                    line_peer(self.lines, d),
                )
            )
        self.across = [
            remote(
                self.mine, self.crossed.at[0], self.sems.at[6, 0], self.sems.at[7, 0], partner()
            )
        ]

    def relay(self):
        for d in range(1, self.lines):
            self.out[d - 1].wait()
            self.across.append(
                remote(
                    self.gathered.at[d],
                    self.crossed.at[d],
                    self.sems.at[6, d],
                    self.sems.at[7, d],
                    partner(),
                )
            )

    def finish(self, put):
        lines = self.lines
        line, side = place()
        rows = self.mine.shape[0]

        def place_block(owner, block):
            put(pl.ds(pl.multiple_of(owner * rows, rows), rows), block.astype(jnp.float32))

        place_block(line * PAIR + side, self.mine[...])
        for d in range(1, lines):
            place_block(lax.rem(line - d + lines, lines) * PAIR + side, self.gathered[d])
        for d in range(lines):
            self.across[d].wait()
            place_block(lax.rem(line - d + lines, lines) * PAIR + (1 - side), self.crossed[d])


def ns_forward(s, m):
    matrix = s.totals[m]
    norm = jnp.sqrt(jnp.sum(matrix * matrix))
    s.current[m] = matrix / (norm + EPS)

    def keep(k, x, gram, poly):
        s.xs[k, m], s.grams[k, m], s.polys[k, m] = x, gram, poly

    def single(k, carry):
        x = rounded(s.current[m])
        gram = times_transpose(x, x)
        gram_r = rounded(gram)
        poly = rounded(C3 * gram + C5 * product(gram_r, gram_r))
        keep(k, x, gram_r, poly)
        s.current[m] = C1 * s.current[m] + product(poly, x)
        return carry

    def precise(k, carry):
        xp = split(s.current[m])
        gram = dot_split(xp, xp, times_transpose)
        gp = split(gram)
        poly = split(C3 * gram + C5 * dot_split(gp, gp, product))
        keep(k, xp[0], gp[0], poly[0])
        s.current[m] = C1 * s.current[m] + dot_split(poly, xp, product)
        return carry

    lax.fori_loop(0, NS_SINGLE, single, 0)
    lax.fori_loop(NS_SINGLE, NS_STEPS, precise, 0)


def ns_backward(s, m):
    s.current[m] = s.adjoint[m]

    def step(i, carry):
        k = NS_STEPS - 1 - i
        grad = s.current[m]
        grad_r, x = rounded(grad), s.xs[k, m]
        dpoly = times_transpose(grad_r, x)
        sym = dpoly + dpoly.T
        twist = product(rounded(sym), s.grams[k, m])
        weight = rounded(C3 * sym + C5 * (twist + twist.T))
        s.current[m] = C1 * grad + product(
            jnp.concatenate([s.polys[k, m], weight], axis=1),
            jnp.concatenate([grad_r, x], axis=0),
        )
        return carry

    lax.fori_loop(0, NS_STEPS, step, 0)
    matrix, grad = s.totals[m], s.current[m]
    norm = jnp.sqrt(jnp.sum(matrix * matrix))
    shifted = norm + EPS
    dot_all = jnp.sum(grad * matrix)
    return grad / shifted - matrix * (dot_all / (norm * shifted * shifted))


OPERANDS = (
    "inputs", "rates", "proj_query", "proj_key", "proj_value", "proj_output",
    "fast_in", "fast_up", "fast_out", "cotangent",
)
RESULTS = (
    "grads_hbm", "rate_hbm", "in_hbm", "up_hbm", "out_hbm",
    "query_hbm", "key_hbm", "value_hbm", "output_hbm",
)


def scratch_of(n, tokens, width, h, f):
    lines = n // PAIR
    rows, wide_rows = h // n, width // n
    bf16, f32 = jnp.bfloat16, jnp.float32
    tile = math.gcd(tokens, 256)
    v = pltpu.VMEM
    return dict(
        x=v((tokens, width), bf16),
        cot=v((tokens, width), bf16),
        x_t=v((width, tokens), bf16),
        cot_t=v((width, tokens), bf16),
        wall=v((width, 3 * h), bf16),
        wo=v((h, width), bf16),
        rates_in=v((tokens // LANES, LANES), f32),
        rate_cols=v((tokens, LANES), f32),
        fin=v((h, f), f32),
        fup=v((h, f), f32),
        fout=v((f, h), f32),
        fout_t=v((h, f), f32),
        b4=v((h, 4 * f), bf16),
        bow=v((h, 2 * f), bf16),
        nw=v((h, 2 * f), bf16),
        no_t=v((h, f), bf16),
        key=v((tokens, h), bf16),
        value=v((tokens, h), bf16),
        scaled=v((tokens, h), bf16),
        key_t=v((h, tokens), bf16),
        scaled_t=v((h, tokens), bf16),
        query=v((tokens, h), bf16),
        back_out=v((tokens, h), bf16),
        pre=v((tokens, 2 * f), f32),
        ups=v((tokens, f), f32),
        work=v((tile, 3 * f), f32),
        hb=v((tokens, 2 * f), bf16),
        g4=v((tokens, 4 * f), bf16),
        hq=v((tokens, f), bf16),
        bpr=v((tokens, 2 * f), bf16),
        grads=v((tokens, 3 * h), bf16),
        orow=v((tokens, h), bf16),
        rate_out=v((tokens // LANES, LANES), f32),
        xs=v((NS_STEPS, COUNT, h, f), bf16),
        grams=v((NS_STEPS, COUNT, h, h), bf16),
        polys=v((NS_STEPS, COUNT, h, h), bf16),
        current=v((COUNT, h, f), f32),
        totals=v((COUNT, h, f), f32),
        adjoint=v((COUNT, h, f), f32),
        gout=v((f, h), f32),
        row_sums=v((GROUPS - 1, wide_rows, h), f32),
        output_sum=v((h, wide_rows), f32),
        part=v((COUNT, n, rows, f), bf16),
        middle=v((COUNT, lines, rows, f), bf16),
        mine=v((COUNT, rows, f), bf16),
        paired=v((ROUNDS, COUNT, lines, rows, f), bf16),
        lined=v((ROUNDS, COUNT, lines, rows, f), bf16),
        gathered=v((ROUNDS, COUNT, lines, rows, f), bf16),
        crossed=v((ROUNDS, COUNT, lines, rows, f), bf16),
        sems=pltpu.SemaphoreType.DMA((ROUNDS, COUNT, 8, lines)),
        row_part=v((GROUPS, n, wide_rows, h), bf16),
        row_paired=v((GROUPS, lines, wide_rows, h), bf16),
        row_middle=v((GROUPS, lines, wide_rows, h), bf16),
        row_lined=v((GROUPS, lines, wide_rows, h), bf16),
        row_sems=pltpu.SemaphoreType.DMA((GROUPS, 4, lines)),
        load_sems=pltpu.SemaphoreType.DMA((8,)),
        x_sems=pltpu.SemaphoreType.DMA((tokens // tile,)),
        cot_sems=pltpu.SemaphoreType.DMA((tokens // tile,)),
        store_sems=pltpu.SemaphoreType.DMA((len(RESULTS),)),
    )


def kernel(n, names, *refs):
    s = SimpleNamespace(**dict(zip(names, refs)))
    lines = n // PAIR
    tokens, width = s.x.shape
    h, f = s.fin.shape
    tile = math.gcd(tokens, 256)
    tiles = tokens // tile
    sub = math.gcd(tile, 32)
    half = math.gcd(f, 256)
    f32 = jnp.float32

    def rows_at(i, size=tile):
        return pl.ds(pl.multiple_of(i * size, size), size)

    def over_tiles(step, first=0, last=tiles):
        def body(i, carry):
            step(i, rows_at(i))
            return carry

        lax.fori_loop(first, last, body, 0)

    def over_subs(step):
        def body(i, carry):
            for j in range(f // half):
                step(i, j * half)
            return carry

        lax.fori_loop(0, tile // sub, body, 0)

    def load(src, dst, sem):
        copy = pltpu.make_async_copy(src, dst, sem)
        copy.start()
        return copy

    def x_copy(i, at):
        return pltpu.make_async_copy(s.inputs.at[at], s.x.at[at], s.x_sems.at[i])

    def cot_copy(i, at):
        return pltpu.make_async_copy(s.cotangent.at[at], s.cot.at[at], s.cot_sems.at[i])

    reduces = [
        [
            Reduce(
                lines, s.part.at[c], s.paired.at[r, c], s.middle.at[c], s.lined.at[r, c],
                s.sems.at[r, c], s.mine.at[c], s.gathered.at[r, c], s.crossed.at[r, c],
            )
            for c in range(COUNT)
        ]
        for r in range(ROUNDS)
    ]
    scatters = [
        Scatter(
            lines, s.row_part.at[g], s.row_paired.at[g], s.row_middle.at[g], s.row_lined.at[g],
            s.row_sems.at[g],
        )
        for g in range(GROUPS)
    ]

    greet(lines)
    x_copy(0, pl.ds(0, tile)).start()
    loads = [
        load(s.proj_key, s.wall.at[:, h : 2 * h], s.load_sems.at[0]),
        load(s.proj_value, s.wall.at[:, 2 * h :], s.load_sems.at[1]),
        load(s.rates, s.rates_in, s.load_sems.at[2]),
        load(s.fast_in, s.fin, s.load_sems.at[3]),
        load(s.fast_up, s.fup, s.load_sems.at[4]),
        load(s.fast_out, s.fout, s.load_sems.at[5]),
    ]
    for i in range(1, tiles):
        x_copy(i, pl.ds(i * tile, tile)).start()
    loads += [
        load(s.proj_query, s.wall.at[:, :h], s.load_sems.at[6]),
        load(s.proj_output, s.wo, s.load_sems.at[7]),
    ]
    for i in range(tiles):
        cot_copy(i, pl.ds(i * tile, tile)).start()

    for copy in loads[:6]:
        copy.wait()
    s.b4[:, 2 * f : 3 * f] = rounded(s.fin[...])
    s.b4[:, 3 * f :] = rounded(s.fup[...])
    s.fout_t[...] = s.fout[...].T
    s.bow[:, f:] = rounded(s.fout_t[...])
    for i in range(tokens // LANES):
        s.rate_cols[i * LANES : (i + 1) * LANES, :] = jnp.broadcast_to(
            s.rates_in[i : i + 1, :], (LANES, LANES)
        ).T

    def rate_of(at, wide):
        return jnp.concatenate([s.rate_cols[at, :]] * (wide // LANES), axis=1)

    def update(i, at):
        x_copy(i, at).wait()
        both = product(s.x[at, :], s.wall[:, h:])
        key = rounded(both[:, :h])
        value = rounded(both[:, h:])
        scaled = rounded(rate_of(at, h) * value.astype(f32))
        s.key[at, :], s.value[at, :], s.scaled[at, :] = key, value, scaled
        s.pre[at, :] = product(key, s.b4[:, 2 * f :])
        s.ups[at, :] = product(scaled, s.bow[:, f:])
        s.key_t[:, at] = key.T
        s.scaled_t[:, at] = scaled.T

        def point(j, col):
            to = pl.ds(pl.multiple_of(i * tile + j * sub, sub), sub)
            pre_in, pre_up = s.pre[to, col : col + half], s.pre[to, f + col : f + col + half]
            up = s.ups[to, col : col + half]
            _, activation, slope = sigmoid_slope(pre_in)
            s.hb[to, col : col + half] = rounded(activation * pre_up)
            s.g4[to, col : col + half] = rounded(up * pre_up * slope)
            s.g4[to, f + col : f + col + half] = rounded(up * activation)

        over_subs(point)

    over_tiles(update)
    greeted(lines)
    now = reduces[0]
    now[0].fill(product(s.key_t[...], s.g4[:, :f]))
    now[0].start()
    now[1].fill(product(s.key_t[...], s.g4[:, f : 2 * f]))
    now[1].start()
    now[2].fill(product(s.scaled_t[...], s.hb[:, :f]))
    now[2].start()

    def total_put(m):
        def put(at, block):
            s.totals[m, at, :] = block

        return put

    def project(i, at):
        s.query[at, :] = rounded(product(s.x[at, :], s.wall[:, :h]))
        cot_copy(i, at).wait()
        s.back_out[at, :] = rounded(times_transpose(s.cot[at, :], s.wo[...]))

    def turn(i, at):
        s.x_t[:, at] = s.x[at, :].T
        s.cot_t[:, at] = s.cot[at, :].T

    for copy in loads[6:]:
        copy.wait()
    now[0].forward()
    over_tiles(project)
    now[1].forward()
    now[0].gather()
    over_tiles(turn)
    now[2].forward()
    now[1].gather()
    now[0].relay()
    now[2].gather()
    now[0].finish(total_put(0))
    now[1].relay()
    ns_forward(s, 0)
    now[2].relay()
    now[1].finish(total_put(1))
    ns_forward(s, 1)
    s.nw[:, :f] = rounded(s.fin[...] + s.current[0])
    s.nw[:, f:] = rounded(s.fup[...] + s.current[1])
    now[2].finish(total_put(2))
    ns_forward(s, 2)
    s.no_t[...] = rounded(s.fout_t[...] + s.current[2])

    def query(i, at):
        s.work[:, : 2 * f] = product(s.query[at, :], s.nw[...])
        s.work[:, 2 * f :] = product(s.back_out[at, :], s.no_t[...])

        def point(j, col):
            here = rows_at(j, sub)
            to = pl.ds(pl.multiple_of(i * tile + j * sub, sub), sub)
            pre_p = s.work[here, col : col + half]
            pre_r = s.work[here, f + col : f + col + half]
            back = s.work[here, 2 * f + col : 2 * f + col + half]
            _, activation, slope = sigmoid_slope(pre_p)
            s.hq[to, col : col + half] = rounded(activation * pre_r)
            s.bpr[to, col : col + half] = rounded(back * pre_r * slope)
            s.bpr[to, f + col : f + col + half] = rounded(back * activation)

        over_subs(point)

    over_tiles(query)
    now = reduces[1]
    now[2].fill(token_sum(s.back_out[...], s.hq[...]))
    now[2].start()
    query_sums = token_sum(s.query[...], s.bpr[...])
    now[0].fill(query_sums)
    now[0].start()
    now[1].fill(query_sums, f)
    now[1].start()

    def adjoint_put(m):
        def put(at, block):
            s.adjoint[m, at, :] = block

        return put

    def query_back(i, at):
        s.grads[at, :h] = rounded(times_transpose(s.bpr[at, :], s.nw[...]))
        s.orow[at, :] = rounded(times_transpose(s.hq[at, :], s.no_t[...]))

    now[2].forward()
    over_tiles(query_back)
    now[0].forward()
    now[2].gather()
    scatters[0].fill(product(s.x_t[...], s.grads[:, :h]))
    now[1].forward()
    now[0].gather()
    now[2].relay()
    scatters[1].fill(product(s.cot_t[...], s.orow[...]))
    now[1].gather()
    now[2].finish(adjoint_put(2))
    now[0].relay()
    s.bow[:, :f] = rounded(ns_backward(s, 2))
    now[1].relay()
    scatters[0].start()
    now[0].finish(adjoint_put(0))
    s.b4[:, :f] = rounded(ns_backward(s, 0))
    scatters[1].start()
    now[1].finish(adjoint_put(1))
    s.b4[:, f : 2 * f] = rounded(ns_backward(s, 1))
    scatters[0].forward()

    def update_back(i, at):
        s.work[:, : 2 * f] = product(s.key[at, :], s.b4[:, : 2 * f])
        s.work[:, 2 * f :] = product(s.scaled[at, :], s.bow[:, :f])

        def point(j, col):
            here = rows_at(j, sub)
            to = pl.ds(pl.multiple_of(i * tile + j * sub, sub), sub)
            press_in = s.work[here, col : col + half]
            press_up = s.work[here, f + col : f + col + half]
            back_hid = s.work[here, 2 * f + col : 2 * f + col + half]
            pre_in, pre_up = s.pre[to, col : col + half], s.pre[to, f + col : f + col + half]
            up = s.ups[to, col : col + half]
            sigma, activation, slope = sigmoid_slope(pre_in)
            rest = 1.0 - sigma
            curvature = sigma * rest * (2.0 + pre_in * (rest - sigma))
            press_slope = press_in * slope
            s.hb[to, f + col : f + col + half] = rounded(press_slope * pre_up + press_up * activation)
            s.g4[to, 3 * f + col : 3 * f + col + half] = rounded(
                press_slope * up + back_hid * activation
            )
            s.g4[to, 2 * f + col : 2 * f + col + half] = rounded(
                press_in * up * pre_up * curvature + (press_up * up + back_hid * pre_up) * slope
            )

        over_subs(point)

    over_tiles(update_back)
    now = reduces[2]
    now[2].fill(product(s.scaled_t[...], s.hb[:, f:]))
    now[2].start()
    now[0].fill(product(s.key_t[...], s.g4[:, 2 * f : 3 * f]))
    now[0].start()
    now[1].fill(product(s.key_t[...], s.g4[:, 3 * f :]))
    now[1].start()
    scatters[1].forward()

    def token_back(i, at):
        back_scaled = times_transpose(s.hb[at, :], s.bow[...])
        weighed = back_scaled * s.value[at, :].astype(f32)
        for t in range(tile // LANES):
            block = weighed[t * LANES : (t + 1) * LANES, :]
            folded = block[:, :LANES]
            for c in range(1, h // LANES):
                folded = folded + block[:, c * LANES : (c + 1) * LANES]
            s.rate_out[pl.ds(i * (tile // LANES) + t, 1), :] = jnp.sum(
                folded.T, axis=0, keepdims=True
            )
        s.grads[at, 2 * h :] = rounded(rate_of(at, h) * back_scaled)
        s.grads[at, h : 2 * h] = rounded(times_transpose(s.g4[at, :], s.b4[...]))

    over_tiles(token_back, 0, tiles // 2)
    now[2].forward()
    over_tiles(token_back, tiles // 2, tiles)
    stores = [
        load(s.grads, s.grads_hbm, s.store_sems.at[0]),
        load(s.rate_out, s.rate_hbm, s.store_sems.at[1]),
    ]
    now[0].forward()
    now[2].gather()
    key_value = product(s.x_t[...], s.grads[:, h:])
    scatters[2].fill(key_value)
    scatters[2].start()
    scatters[3].fill(key_value, h)
    scatters[3].start()
    now[1].forward()
    now[0].gather()
    now[2].relay()
    now[1].gather()
    now[0].relay()
    scatters[2].forward()
    now[1].relay()
    scatters[3].forward()

    def sum_put(m):
        def put(at, block):
            s.totals[m, at, :] = s.adjoint[m, at, :] + block

        return put

    s.row_sums[0] = scatters[0].total()
    stores.append(load(s.row_sums.at[0], s.query_hbm, s.store_sems.at[5]))
    s.output_sum[...] = scatters[1].total().T
    stores.append(load(s.output_sum, s.output_hbm, s.store_sems.at[8]))
    now[2].finish(sum_put(2))
    s.gout[...] = s.totals[2].T
    stores.append(load(s.gout, s.out_hbm, s.store_sems.at[4]))
    now[0].finish(sum_put(0))
    stores.append(load(s.totals.at[0], s.in_hbm, s.store_sems.at[2]))
    s.row_sums[1] = scatters[2].total()
    stores.append(load(s.row_sums.at[1], s.key_hbm, s.store_sems.at[6]))
    s.row_sums[2] = scatters[3].total()
    stores.append(load(s.row_sums.at[2], s.value_hbm, s.store_sems.at[7]))
    now[1].finish(sum_put(1))
    stores.append(load(s.totals.at[1], s.up_hbm, s.store_sems.at[3]))
    for copy in stores:
        copy.wait()


def last_kernel(grads, proj_query, proj_key, proj_value, *rest):
    back_inputs, copies = rest[len(rest) // 2], rest[: len(rest) // 2]
    weights = jnp.concatenate([proj_query[...], proj_key[...], proj_value[...]], axis=1)
    back_inputs[...] = rounded(times_transpose(grads[...], weights))
    for src, dst in zip(copies, rest[len(rest) // 2 + 1 :]):
        dst[...] = src[...]


def body(n, *operands):
    inputs, rates, fast_in = operands[0], operands[1], operands[6]
    tokens, width = inputs.shape
    h, f = fast_in.shape
    wide_rows = width // n
    bf16, f32 = jnp.bfloat16, jnp.float32
    outs = [
        ((tokens, 3 * h), bf16),
        ((tokens // LANES, LANES), f32),
        ((h, f), f32),
        ((h, f), f32),
        ((f, h), f32),
        ((wide_rows, h), f32),
        ((wide_rows, h), f32),
        ((wide_rows, h), f32),
        ((h, wide_rows), f32),
    ]
    scratch = scratch_of(n, tokens, width, h, f)
    anywhere = pl.BlockSpec(memory_space=pl.ANY)
    operands = list(operands)
    operands[1] = rates.reshape(tokens // LANES, LANES)
    results = pl.pallas_call(
        functools.partial(kernel, n, OPERANDS + RESULTS + tuple(scratch)),
        out_shape=[jax.ShapeDtypeStruct(shape, kind) for shape, kind in outs],
        in_specs=[anywhere] * len(operands),
        out_specs=[anywhere] * len(outs),
        scratch_shapes=list(scratch.values()),
        compiler_params=pltpu.CompilerParams(
            collective_id=0, has_side_effects=True, vmem_limit_bytes=VMEM_LIMIT
        ),
    )(*operands)

    grads, rest = results[0], results[1:]
    tile = math.gcd(tokens, 256)
    whole = lambda array: pl.BlockSpec(array.shape, lambda i: (0,) * array.ndim)
    token_block = pl.BlockSpec((tile, width), lambda i: (i, 0))
    return pl.pallas_call(
        lambda *refs: last_kernel(*refs),
        grid=(tokens // tile,),
        out_shape=[jax.ShapeDtypeStruct((tokens, width), bf16)]
        + [jax.ShapeDtypeStruct(r.shape, r.dtype) for r in rest],
        in_specs=[pl.BlockSpec((tile, 3 * h), lambda i: (i, 0))]
        + [whole(w) for w in operands[2:5]]
        + [whole(r) for r in rest],
        out_specs=[token_block] + [whole(r) for r in rest],
    )(grads, *operands[2:5], *rest)


def solution(mesh):
    n = mesh.shape["seq"]

    def step(*operands):
        outs = body(n, *operands)
        return (outs[0], outs[1].reshape(-1)) + tuple(outs[2:])

    in_specs = (
        P(("batch", "seq"), None),
        P(("batch", "seq")),
        P(),
        P(),
        P(),
        P(),
        P(),
        P(),
        P(),
        P(("batch", "seq"), None),
    )
    out_specs = (
        P(("batch", "seq"), None),
        P(("batch", "seq")),
        P("batch", None),
        P("batch", None),
        P("batch", None),
        P("seq", "batch"),
        P("seq", "batch"),
        P("seq", "batch"),
        P("batch", "seq"),
    )
    return jax.shard_map(
        step, mesh=mesh, in_specs=in_specs, out_specs=out_specs, check_vma=False
    )
```

```python
import functools
import math
from types import SimpleNamespace

import jax
import jax.numpy as jnp
from jax import lax
from jax.experimental import pallas as pl
from jax.experimental.pallas import tpu as pltpu
from jax.sharding import PartitionSpec as P

NS_STEPS = 5
NS_SINGLE = 2
C1, C3, C5 = 3.4445, -4.775, 2.0315
EPS = 1e-07
MESH = pl.DeviceIdType.MESH
VMEM_LIMIT = 66_000_000
PAIR = 2
COUNT = 3
LANES = 128
ROUNDS = 3
GROUPS = 4
PIECE = 384 * 1024


def rounded(value):
    return value.astype(jnp.bfloat16)


def product(left, right):
    return jnp.dot(left, right, preferred_element_type=jnp.float32)


def token_sum(left, right):
    return lax.dot_general(
        left, right, (((0,), (0,)), ((), ())), preferred_element_type=jnp.float32
    )


def times_transpose(left, right):
    return lax.dot_general(
        left, right, (((1,), (1,)), ((), ())), preferred_element_type=jnp.float32
    )


def sigmoid_slope(pre_act):
    sigma = jax.nn.sigmoid(pre_act)
    return sigma, pre_act * sigma, sigma * (1.0 + pre_act * (1.0 - sigma))


def split(value):
    high = rounded(value)
    return (high, rounded(value - high.astype(jnp.float32)))


def place():
    me = lax.axis_index("seq")
    return me // PAIR, me % PAIR


def remote(src, dst, send, recv, device):
    copy = pltpu.make_async_remote_copy(
        src_ref=src,
        dst_ref=dst,
        send_sem=send,
        recv_sem=recv,
        device_id={"seq": device},
        device_id_type=MESH,
    )
    copy.start()
    return copy


def line_peer(lines, d):
    line, side = place()
    return lax.rem(line + d, lines) * PAIR + side


def partner():
    line, side = place()
    return line * PAIR + (1 - side)


def greet(lines):
    barrier = pltpu.get_barrier_semaphore()
    for peer in [partner()] + [line_peer(lines, d) for d in range(1, lines)]:
        pl.semaphore_signal(barrier, inc=1, device_id={"seq": peer}, device_id_type=MESH)


def greeted(lines):
    pl.semaphore_wait(pltpu.get_barrier_semaphore(), lines)


class Scatter:
    def __init__(self, lines, part, paired, middle, lined, sems):
        self.lines = lines
        self.part, self.paired, self.middle, self.lined = part, paired, middle, lined
        self.sems = sems

    def fill(self, total, at=0):
        n, rows, wide = self.part.shape
        for j in range(n):
            self.part[j] = rounded(total[j * rows : (j + 1) * rows, at : at + wide])

    def start(self):
        lines = self.lines
        line, side = place()
        self.pairs = {}
        for d in list(range(1, lines)) + [0]:
            to = lax.rem(line + d, lines)
            self.pairs[d] = remote(
                self.part.at[to * PAIR + (1 - side)],
                self.paired.at[d],
                self.sems.at[0, d],
                self.sems.at[1, d],
                partner(),
            )

    def forward(self):
        lines = self.lines
        line, side = place()
        self.sent = []
        for d in range(1, lines):
            to = lax.rem(line + d, lines)
            self.pairs[d].wait()
            self.middle[d] = rounded(
                self.part[to * PAIR + side].astype(jnp.float32)
                + self.paired[d].astype(jnp.float32)
            )
            self.sent.append(
                remote(
                    self.middle.at[d],
                    self.lined.at[d],
                    self.sems.at[2, d],
                    self.sems.at[3, d],
                    to * PAIR + side,
                )
            )

    def total(self):
        self.pairs[0].wait()
        me = lax.axis_index("seq")
        total = self.part[me].astype(jnp.float32) + self.paired[0].astype(jnp.float32)
        for d, copy in zip(range(1, self.lines), self.sent):
            copy.wait()
            total = total + self.lined[d].astype(jnp.float32)
        return total


class Reduce(Scatter):
    def __init__(self, lines, part, paired, middle, lined, sems, mine, gathered, crossed):
        super().__init__(lines, part, paired, middle, lined, sems)
        self.mine, self.gathered, self.crossed = mine, gathered, crossed

    def gather(self):
        self.mine[...] = rounded(self.total())
        self.out = []
        for d in range(1, self.lines):
            self.out.append(
                remote(
                    self.mine,
                    self.gathered.at[d],
                    self.sems.at[4, d],
                    self.sems.at[5, d],
                    line_peer(self.lines, d),
                )
            )
        self.across = [
            remote(
                self.mine, self.crossed.at[0], self.sems.at[6, 0], self.sems.at[7, 0], partner()
            )
        ]

    def relay(self):
        for d in range(1, self.lines):
            self.out[d - 1].wait()
            self.across.append(
                remote(
                    self.gathered.at[d],
                    self.crossed.at[d],
                    self.sems.at[6, d],
                    self.sems.at[7, d],
                    partner(),
                )
            )

    def finish(self, put):
        lines = self.lines
        line, side = place()
        rows = self.mine.shape[0]

        def place_block(owner, block):
            put(pl.ds(pl.multiple_of(owner * rows, rows), rows), block.astype(jnp.float32))

        place_block(line * PAIR + side, self.mine[...])
        for d in range(1, lines):
            place_block(lax.rem(line - d + lines, lines) * PAIR + side, self.gathered[d])
        for d in range(lines):
            self.across[d].wait()
            place_block(lax.rem(line - d + lines, lines) * PAIR + (1 - side), self.crossed[d])


def squared(parts, dot):
    along = 0 if dot is times_transpose else 1
    both = dot(parts[0], jnp.concatenate(parts, axis=along))
    wide = both.shape[1] // 2
    return both[:, :wide] + (both[:, wide:] + both[:, wide:].T)


def ns_forward(s):
    each = range(COUNT)
    for m in each:
        matrix = s.totals[m]
        s.current[m] = matrix / (jnp.sqrt(jnp.sum(matrix * matrix)) + EPS)

    def keep(k, m, x, gram, poly):
        s.xs[k, m], s.grams[k, m], s.polys[k, m] = x, gram, poly

    def single(k, carry):
        xs = [rounded(s.current[m]) for m in each]
        grams = [times_transpose(x, x) for x in xs]
        grams_r = [rounded(gram) for gram in grams]
        polys = [rounded(C3 * g + C5 * product(r, r)) for g, r in zip(grams, grams_r)]
        for m in each:
            keep(k, m, xs[m], grams_r[m], polys[m])
            s.current[m] = C1 * s.current[m] + product(polys[m], xs[m])
        return carry

    def precise(k, carry):
        xs = [split(s.current[m]) for m in each]
        grams = [squared(x, times_transpose) for x in xs]
        parts = [split(gram) for gram in grams]
        polys = [split(C3 * g + C5 * squared(p, product)) for g, p in zip(grams, parts)]
        for m in each:
            keep(k, m, xs[m][0], parts[m][0], polys[m][0])
            tall = product(jnp.concatenate(polys[m], axis=0), xs[m][0])
            rows = tall.shape[0] // 2
            s.current[m] = (
                C1 * s.current[m]
                + (tall[:rows] + tall[rows:])
                + product(polys[m][0], xs[m][1])
            )
        return carry

    lax.fori_loop(0, NS_SINGLE, single, 0)
    lax.fori_loop(NS_SINGLE, NS_STEPS, precise, 0)


def ns_backward(s):
    each = range(COUNT)
    for m in each:
        s.current[m] = s.adjoint[m]

    def step(i, carry):
        k = NS_STEPS - 1 - i
        grads = [rounded(s.current[m]) for m in each]
        dpolys = [times_transpose(grads[m], s.xs[k, m]) for m in each]
        syms = [dpoly + dpoly.T for dpoly in dpolys]
        twists = [product(rounded(syms[m]), s.grams[k, m]) for m in each]
        weights = [rounded(C3 * sym + C5 * (t + t.T)) for sym, t in zip(syms, twists)]
        for m in each:
            s.current[m] = C1 * s.current[m] + product(
                jnp.concatenate([s.polys[k, m], weights[m]], axis=1),
                jnp.concatenate([grads[m], s.xs[k, m]], axis=0),
            )
        return carry

    lax.fori_loop(0, NS_STEPS, step, 0)
    results = []
    for m in each:
        matrix, grad = s.totals[m], s.current[m]
        norm = jnp.sqrt(jnp.sum(matrix * matrix))
        shifted = norm + EPS
        dot_all = jnp.sum(grad * matrix)
        results.append(
            rounded(grad / shifted - matrix * (dot_all / (norm * shifted * shifted)))
        )
    return results


OPERANDS = (
    "inputs", "rates", "proj_query", "proj_key", "proj_value", "proj_output",
    "fast_in", "fast_up", "fast_out", "cotangent",
)
RESULTS = (
    "back_hbm", "rate_hbm", "in_hbm", "up_hbm", "out_hbm",
    "query_hbm", "key_hbm", "value_hbm", "output_hbm",
)


def scratch_of(n, tokens, width, h, f):
    lines = n // PAIR
    rows, wide_rows = h // n, width // n
    bf16, f32 = jnp.bfloat16, jnp.float32
    tile = math.gcd(tokens, 256)
    v = pltpu.VMEM
    return dict(
        x=v((tokens, width), bf16),
        cot=v((tokens, width), bf16),
        x_t=v((width, tokens), bf16),
        cot_t=v((width, tokens), bf16),
        wall=v((width, 3 * h), bf16),
        wo=v((h, width), bf16),
        rates_in=v((tokens // LANES, LANES), f32),
        rate_cols=v((tokens, LANES), f32),
        fin=v((h, f), f32),
        fup=v((h, f), f32),
        fout=v((f, h), f32),
        fout_t=v((h, f), f32),
        b4=v((h, 4 * f), bf16),
        bow=v((h, 2 * f), bf16),
        nw=v((h, 2 * f), bf16),
        no_t=v((h, f), bf16),
        key=v((tokens, h), bf16),
        value=v((tokens, h), bf16),
        scaled=v((tokens, h), bf16),
        key_t=v((h, tokens), bf16),
        scaled_t=v((h, tokens), bf16),
        query=v((tokens, h), bf16),
        back_out=v((tokens, h), bf16),
        pre=v((tokens, 2 * f), f32),
        ups=v((tokens, f), f32),
        work=v((tile, 3 * f), f32),
        hb=v((tokens, 2 * f), bf16),
        g4=v((tokens, 4 * f), bf16),
        hq=v((tokens, f), bf16),
        bpr=v((tokens, 2 * f), bf16),
        grads=v((tokens, 3 * h), bf16),
        orow=v((tokens, h), bf16),
        rate_out=v((tokens // LANES, LANES), f32),
        xs=v((NS_STEPS, COUNT, h, f), bf16),
        grams=v((NS_STEPS, COUNT, h, h), bf16),
        polys=v((NS_STEPS, COUNT, h, h), bf16),
        current=v((COUNT, h, f), f32),
        totals=v((COUNT, h, f), f32),
        adjoint=v((COUNT, h, f), f32),
        gout=v((f, h), f32),
        row_sums=v((GROUPS, wide_rows, h), f32),
        part=v((COUNT, n, rows, f), bf16),
        middle=v((COUNT, lines, rows, f), bf16),
        mine=v((COUNT, rows, f), bf16),
        paired=v((ROUNDS, COUNT, lines, rows, f), bf16),
        lined=v((ROUNDS, COUNT, lines, rows, f), bf16),
        gathered=v((ROUNDS, COUNT, lines, rows, f), bf16),
        crossed=v((ROUNDS, COUNT, lines, rows, f), bf16),
        sems=pltpu.SemaphoreType.DMA((ROUNDS, COUNT, 8, lines)),
        row_part=v((GROUPS, n, wide_rows, h), bf16),
        row_paired=v((GROUPS, lines, wide_rows, h), bf16),
        row_middle=v((GROUPS, lines, wide_rows, h), bf16),
        row_lined=v((GROUPS, lines, wide_rows, h), bf16),
        row_sems=pltpu.SemaphoreType.DMA((GROUPS, 4, lines)),
        load_sems=pltpu.SemaphoreType.DMA((8,)),
        x_sems=pltpu.SemaphoreType.DMA((tokens // tile,)),
        cot_sems=pltpu.SemaphoreType.DMA((tokens // tile,)),
        store_sems=pltpu.SemaphoreType.DMA((len(RESULTS),)),
    )


def kernel(n, names, *refs):
    s = SimpleNamespace(**dict(zip(names, refs)))
    lines = n // PAIR
    tokens, width = s.x.shape
    h, f = s.fin.shape
    tile = math.gcd(tokens, 256)
    tiles = tokens // tile
    sub = math.gcd(tile, 32)
    half = math.gcd(f, 256)
    f32 = jnp.float32

    def rows_at(i, size=tile):
        return pl.ds(pl.multiple_of(i * size, size), size)

    def over_tiles(step, first=0, last=tiles):
        def body(i, carry):
            step(i, rows_at(i))
            return carry

        lax.fori_loop(first, last, body, 0)

    def over_subs(step):
        def body(i, carry):
            for j in range(f // half):
                step(i, j * half)
            return carry

        lax.fori_loop(0, tile // sub, body, 0)

    def load(src, dst, sem):
        copy = pltpu.make_async_copy(src, dst, sem)
        copy.start()
        return copy

    def x_copy(i, at):
        return pltpu.make_async_copy(s.inputs.at[at], s.x.at[at], s.x_sems.at[i])

    def cot_copy(i, at):
        return pltpu.make_async_copy(s.cotangent.at[at], s.cot.at[at], s.cot_sems.at[i])

    reduces = [
        [
            Reduce(
                lines, s.part.at[c], s.paired.at[r, c], s.middle.at[c], s.lined.at[r, c],
                s.sems.at[r, c], s.mine.at[c], s.gathered.at[r, c], s.crossed.at[r, c],
            )
            for c in range(COUNT)
        ]
        for r in range(ROUNDS)
    ]
    scatters = [
        Scatter(
            lines, s.row_part.at[g], s.row_paired.at[g], s.row_middle.at[g], s.row_lined.at[g],
            s.row_sems.at[g],
        )
        for g in range(GROUPS)
    ]

    greet(lines)
    x_copy(0, pl.ds(0, tile)).start()
    loads = [
        load(s.proj_key, s.wall.at[:, h : 2 * h], s.load_sems.at[0]),
        load(s.proj_value, s.wall.at[:, 2 * h :], s.load_sems.at[1]),
        load(s.rates, s.rates_in, s.load_sems.at[2]),
        load(s.fast_in, s.fin, s.load_sems.at[3]),
        load(s.fast_up, s.fup, s.load_sems.at[4]),
        load(s.fast_out, s.fout, s.load_sems.at[5]),
    ]
    for i in range(1, tiles):
        x_copy(i, pl.ds(i * tile, tile)).start()
    loads += [
        load(s.proj_query, s.wall.at[:, :h], s.load_sems.at[6]),
        load(s.proj_output, s.wo, s.load_sems.at[7]),
    ]
    for i in range(tiles):
        cot_copy(i, pl.ds(i * tile, tile)).start()

    for copy in loads[:6]:
        copy.wait()
    s.b4[:, 2 * f : 3 * f] = rounded(s.fin[...])
    s.b4[:, 3 * f :] = rounded(s.fup[...])
    s.fout_t[...] = s.fout[...].T
    s.bow[:, f:] = rounded(s.fout_t[...])
    for i in range(tokens // LANES):
        s.rate_cols[i * LANES : (i + 1) * LANES, :] = jnp.broadcast_to(
            s.rates_in[i : i + 1, :], (LANES, LANES)
        ).T

    def rate_of(at, wide):
        return jnp.concatenate([s.rate_cols[at, :]] * (wide // LANES), axis=1)

    def update(i, at):
        x_copy(i, at).wait()
        both = product(s.x[at, :], s.wall[:, h:])
        key = rounded(both[:, :h])
        value = rounded(both[:, h:])
        scaled = rounded(rate_of(at, h) * value.astype(f32))
        s.key[at, :], s.value[at, :], s.scaled[at, :] = key, value, scaled
        s.pre[at, :] = product(key, s.b4[:, 2 * f :])
        s.ups[at, :] = product(scaled, s.bow[:, f:])
        s.key_t[:, at] = key.T
        s.scaled_t[:, at] = scaled.T

        def point(j, col):
            to = pl.ds(pl.multiple_of(i * tile + j * sub, sub), sub)
            pre_in, pre_up = s.pre[to, col : col + half], s.pre[to, f + col : f + col + half]
            up = s.ups[to, col : col + half]
            _, activation, slope = sigmoid_slope(pre_in)
            s.hb[to, col : col + half] = rounded(activation * pre_up)
            s.g4[to, col : col + half] = rounded(up * pre_up * slope)
            s.g4[to, f + col : f + col + half] = rounded(up * activation)

        over_subs(point)

    over_tiles(update)
    greeted(lines)
    now = reduces[0]
    now[0].fill(product(s.key_t[...], s.g4[:, :f]))
    now[0].start()
    now[1].fill(product(s.key_t[...], s.g4[:, f : 2 * f]))
    now[1].start()
    now[2].fill(product(s.scaled_t[...], s.hb[:, :f]))
    now[2].start()

    def total_put(m):
        def put(at, block):
            s.totals[m, at, :] = block

        return put

    def project(i, at):
        s.query[at, :] = rounded(product(s.x[at, :], s.wall[:, :h]))
        cot_copy(i, at).wait()
        s.back_out[at, :] = rounded(times_transpose(s.cot[at, :], s.wo[...]))

    def turn(i, at):
        s.x_t[:, at] = s.x[at, :].T
        s.cot_t[:, at] = s.cot[at, :].T

    for copy in loads[6:]:
        copy.wait()
    now[0].forward()
    over_tiles(project)
    now[1].forward()
    now[0].gather()
    over_tiles(turn)
    now[2].forward()
    now[1].gather()
    now[0].relay()
    now[2].gather()
    now[1].relay()
    now[2].relay()
    for m in range(COUNT):
        now[m].finish(total_put(m))
    ns_forward(s)
    s.nw[:, :f] = rounded(s.fin[...] + s.current[0])
    s.nw[:, f:] = rounded(s.fup[...] + s.current[1])
    s.no_t[...] = rounded(s.fout_t[...] + s.current[2])

    def query(i, at):
        s.work[:, : 2 * f] = product(s.query[at, :], s.nw[...])
        s.work[:, 2 * f :] = product(s.back_out[at, :], s.no_t[...])

        def point(j, col):
            here = rows_at(j, sub)
            to = pl.ds(pl.multiple_of(i * tile + j * sub, sub), sub)
            pre_p = s.work[here, col : col + half]
            pre_r = s.work[here, f + col : f + col + half]
            back = s.work[here, 2 * f + col : 2 * f + col + half]
            _, activation, slope = sigmoid_slope(pre_p)
            s.hq[to, col : col + half] = rounded(activation * pre_r)
            s.bpr[to, col : col + half] = rounded(back * pre_r * slope)
            s.bpr[to, f + col : f + col + half] = rounded(back * activation)

        over_subs(point)

    over_tiles(query)
    now = reduces[1]
    now[2].fill(token_sum(s.back_out[...], s.hq[...]))
    now[2].start()
    query_sums = token_sum(s.query[...], s.bpr[...])
    now[0].fill(query_sums)
    now[0].start()
    now[1].fill(query_sums, f)
    now[1].start()

    def adjoint_put(m):
        def put(at, block):
            s.adjoint[m, at, :] = block

        return put

    def query_back(i, at):
        s.grads[at, :h] = rounded(times_transpose(s.bpr[at, :], s.nw[...]))
        s.orow[at, :] = rounded(times_transpose(s.hq[at, :], s.no_t[...]))

    now[2].forward()
    over_tiles(query_back)
    now[0].forward()
    now[2].gather()
    scatters[0].fill(product(s.x_t[...], s.grads[:, :h]))
    now[1].forward()
    now[0].gather()
    now[2].relay()
    scatters[1].fill(product(s.cot_t[...], s.orow[...]))
    now[1].gather()
    now[0].relay()
    now[1].relay()
    scatters[0].start()
    scatters[1].start()
    for m in (2, 0, 1):
        now[m].finish(adjoint_put(m))
    s.b4[:, :f], s.b4[:, f : 2 * f], s.bow[:, :f] = ns_backward(s)
    scatters[0].forward()

    def update_back(i, at):
        s.work[:, : 2 * f] = product(s.key[at, :], s.b4[:, : 2 * f])
        s.work[:, 2 * f :] = product(s.scaled[at, :], s.bow[:, :f])

        def point(j, col):
            here = rows_at(j, sub)
            to = pl.ds(pl.multiple_of(i * tile + j * sub, sub), sub)
            press_in = s.work[here, col : col + half]
            press_up = s.work[here, f + col : f + col + half]
            back_hid = s.work[here, 2 * f + col : 2 * f + col + half]
            pre_in, pre_up = s.pre[to, col : col + half], s.pre[to, f + col : f + col + half]
            up = s.ups[to, col : col + half]
            sigma, activation, slope = sigmoid_slope(pre_in)
            rest = 1.0 - sigma
            curvature = sigma * rest * (2.0 + pre_in * (rest - sigma))
            press_slope = press_in * slope
            s.hb[to, f + col : f + col + half] = rounded(press_slope * pre_up + press_up * activation)
            s.g4[to, 3 * f + col : 3 * f + col + half] = rounded(
                press_slope * up + back_hid * activation
            )
            s.g4[to, 2 * f + col : 2 * f + col + half] = rounded(
                press_in * up * pre_up * curvature + (press_up * up + back_hid * pre_up) * slope
            )

        over_subs(point)

    over_tiles(update_back)
    now = reduces[2]
    now[2].fill(product(s.scaled_t[...], s.hb[:, f:]))
    now[2].start()
    now[0].fill(product(s.key_t[...], s.g4[:, 2 * f : 3 * f]))
    now[0].start()
    now[1].fill(product(s.key_t[...], s.g4[:, 3 * f :]))
    now[1].start()
    scatters[1].forward()

    def token_back(i, at):
        back_scaled = times_transpose(s.hb[at, :], s.bow[...])
        weighed = back_scaled * s.value[at, :].astype(f32)
        for t in range(tile // LANES):
            block = weighed[t * LANES : (t + 1) * LANES, :]
            folded = block[:, :LANES]
            for c in range(1, h // LANES):
                folded = folded + block[:, c * LANES : (c + 1) * LANES]
            s.rate_out[pl.ds(i * (tile // LANES) + t, 1), :] = jnp.sum(
                folded.T, axis=0, keepdims=True
            )
        s.grads[at, 2 * h :] = rounded(rate_of(at, h) * back_scaled)
        s.grads[at, h : 2 * h] = rounded(times_transpose(s.g4[at, :], s.b4[...]))

    over_tiles(token_back, 0, tiles // 2)
    now[2].forward()
    over_tiles(token_back, tiles // 2, tiles)
    stores = [
        load(s.rate_out, s.rate_hbm, s.store_sems.at[1]),
    ]
    now[0].forward()
    now[2].gather()
    key_value = product(s.x_t[...], s.grads[:, h:])
    scatters[2].fill(key_value)
    scatters[2].start()
    scatters[3].fill(key_value, h)
    scatters[3].start()
    now[1].forward()
    now[0].gather()

    def inputs_back(i, at):
        s.cot[at, :] = rounded(times_transpose(s.grads[at, :], s.wall[...]))

    over_tiles(inputs_back)
    stores.append(load(s.cot, s.back_hbm, s.store_sems.at[0]))
    now[2].relay()
    now[1].gather()
    now[0].relay()
    scatters[2].forward()
    now[1].relay()
    scatters[3].forward()

    def sum_put(m):
        def put(at, block):
            s.totals[m, at, :] = s.adjoint[m, at, :] + block

        return put

    for g, (to, sem) in enumerate(((s.query_hbm, 5), (s.output_hbm, 8))):
        s.row_sums[g] = scatters[g].total()
        stores.append(load(s.row_sums.at[g], to, s.store_sems.at[sem]))
    now[2].finish(sum_put(2))
    s.gout[...] = s.totals[2].T
    stores.append(load(s.gout, s.out_hbm, s.store_sems.at[4]))
    now[0].finish(sum_put(0))
    stores.append(load(s.totals.at[0], s.in_hbm, s.store_sems.at[2]))
    for g, (to, sem) in ((2, (s.key_hbm, 6)), (3, (s.value_hbm, 7))):
        s.row_sums[g] = scatters[g].total()
        stores.append(load(s.row_sums.at[g], to, s.store_sems.at[sem]))
    now[1].finish(sum_put(1))
    stores.append(load(s.totals.at[1], s.up_hbm, s.store_sems.at[3]))
    for copy in stores:
        copy.wait()


def pieces_of(shape, kind):
    size = math.prod(shape) * jnp.dtype(kind).itemsize
    count = max(1, min(size // PIECE, shape[0] // LANES))
    while shape[0] % (16 * count) and count > 1:
        count -= 1
    step = shape[0] // count
    return [pl.ds(i * step, step) for i in range(count)]


def copy_kernel(count, *refs):
    sources, targets, holds = (refs[i * count : (i + 1) * count] for i in range(3))
    sems = refs[-1]
    moves = [
        (src.at[at], hold.at[at], dst.at[at])
        for src, dst, hold in zip(sources, targets, holds)
        for at in pieces_of(src.shape, src.dtype)
    ]
    loads = [
        pltpu.make_async_copy(src, hold, sems.at[0, i])
        for i, (src, hold, _) in enumerate(moves)
    ]
    stores = [
        pltpu.make_async_copy(hold, dst, sems.at[1, i])
        for i, (_, hold, dst) in enumerate(moves)
    ]
    for load in loads:
        load.start()
    for load, store in zip(loads, stores):
        load.wait()
        store.start()
    for store in stores:
        store.wait()


def body(n, *operands):
    inputs, rates, fast_in = operands[0], operands[1], operands[6]
    tokens, width = inputs.shape
    h, f = fast_in.shape
    wide_rows = width // n
    bf16, f32 = jnp.bfloat16, jnp.float32
    outs = [
        ((tokens, width), bf16),
        ((tokens // LANES, LANES), f32),
        ((h, f), f32),
        ((h, f), f32),
        ((f, h), f32),
        ((wide_rows, h), f32),
        ((wide_rows, h), f32),
        ((wide_rows, h), f32),
        ((wide_rows, h), f32),
    ]
    scratch = scratch_of(n, tokens, width, h, f)
    anywhere = pl.BlockSpec(memory_space=pl.ANY)
    operands = list(operands)
    operands[1] = rates.reshape(tokens // LANES, LANES)
    results = pl.pallas_call(
        functools.partial(kernel, n, OPERANDS + RESULTS + tuple(scratch)),
        out_shape=[jax.ShapeDtypeStruct(shape, kind) for shape, kind in outs],
        in_specs=[anywhere] * len(operands),
        out_specs=[anywhere] * len(outs),
        scratch_shapes=list(scratch.values()),
        compiler_params=pltpu.CompilerParams(
            collective_id=0, has_side_effects=True, vmem_limit_bytes=VMEM_LIMIT
        ),
    )(*operands)

    moves = sum(len(pieces_of(shape, kind)) for shape, kind in outs)
    return pl.pallas_call(
        functools.partial(copy_kernel, len(outs)),
        out_shape=[jax.ShapeDtypeStruct(shape, kind) for shape, kind in outs],
        in_specs=[anywhere] * len(outs),
        out_specs=[anywhere] * len(outs),
        scratch_shapes=[pltpu.VMEM(shape, kind) for shape, kind in outs]
        + [pltpu.SemaphoreType.DMA((2, moves))],
    )(*results)


def solution(mesh):
    n = mesh.shape["seq"]

    def step(*operands):
        outs = body(n, *operands)
        return (outs[0], outs[1].reshape(-1)) + tuple(outs[2:8]) + (outs[8].T,)

    in_specs = (
        P(("batch", "seq"), None),
        P(("batch", "seq")),
        P(),
        P(),
        P(),
        P(),
        P(),
        P(),
        P(),
        P(("batch", "seq"), None),
    )
    out_specs = (
        P(("batch", "seq"), None),
        P(("batch", "seq")),
        P("batch", None),
        P("batch", None),
        P("batch", None),
        P("seq", "batch"),
        P("seq", "batch"),
        P("seq", "batch"),
        P("batch", "seq"),
    )
    return jax.shard_map(
        step, mesh=mesh, in_specs=in_specs, out_specs=out_specs, check_vma=False
    )
```

```python
import functools
import math
from types import SimpleNamespace

import jax
import jax.numpy as jnp
from jax import lax
from jax.experimental import pallas as pl
from jax.experimental.pallas import tpu as pltpu
from jax.sharding import PartitionSpec as P

NS_STEPS = 5
NS_SINGLE = 2
C1, C3, C5 = 3.4445, -4.775, 2.0315
EPS = 1e-07
MESH = pl.DeviceIdType.MESH
VMEM_LIMIT = 66_000_000
PAIR = 2
COUNT = 3
LANES = 128
ROUNDS = 3
GROUPS = 4
PIECE = 384 * 1024


def rounded(value):
    return value.astype(jnp.bfloat16)


def product(left, right):
    return jnp.dot(left, right, preferred_element_type=jnp.float32)


def token_sum(left, right):
    return lax.dot_general(
        left, right, (((0,), (0,)), ((), ())), preferred_element_type=jnp.float32
    )


def times_transpose(left, right):
    return lax.dot_general(
        left, right, (((1,), (1,)), ((), ())), preferred_element_type=jnp.float32
    )


def sigmoid_slope(pre_act):
    sigma = jax.nn.sigmoid(pre_act)
    return sigma, pre_act * sigma, sigma * (1.0 + pre_act * (1.0 - sigma))


def split(value):
    high = rounded(value)
    return (high, rounded(value - high.astype(jnp.float32)))


def place():
    me = lax.axis_index("seq")
    return me // PAIR, me % PAIR


def remote(src, dst, send, recv, device):
    copy = pltpu.make_async_remote_copy(
        src_ref=src,
        dst_ref=dst,
        send_sem=send,
        recv_sem=recv,
        device_id={"seq": device},
        device_id_type=MESH,
    )
    copy.start()
    return copy


def line_peer(lines, d):
    line, side = place()
    return lax.rem(line + d, lines) * PAIR + side


def partner():
    line, side = place()
    return line * PAIR + (1 - side)


def greet(lines):
    barrier = pltpu.get_barrier_semaphore()
    for peer in [partner()] + [line_peer(lines, d) for d in range(1, lines)]:
        pl.semaphore_signal(barrier, inc=1, device_id={"seq": peer}, device_id_type=MESH)


def greeted(lines):
    pl.semaphore_wait(pltpu.get_barrier_semaphore(), lines)


class Scatter:
    def __init__(self, lines, part, paired, middle, lined, sems):
        self.lines = lines
        self.part, self.paired, self.middle, self.lined = part, paired, middle, lined
        self.sems = sems

    def fill(self, total, at=0):
        n, rows, wide = self.part.shape
        for j in range(n):
            self.part[j] = rounded(total[j * rows : (j + 1) * rows, at : at + wide])

    def start(self):
        lines = self.lines
        line, side = place()
        self.pairs = {}
        for d in list(range(1, lines)) + [0]:
            to = lax.rem(line + d, lines)
            self.pairs[d] = remote(
                self.part.at[to * PAIR + (1 - side)],
                self.paired.at[d],
                self.sems.at[0, d],
                self.sems.at[1, d],
                partner(),
            )

    def forward(self):
        lines = self.lines
        line, side = place()
        self.sent = []
        for d in range(1, lines):
            to = lax.rem(line + d, lines)
            self.pairs[d].wait()
            self.middle[d] = rounded(
                self.part[to * PAIR + side].astype(jnp.float32)
                + self.paired[d].astype(jnp.float32)
            )
            self.sent.append(
                remote(
                    self.middle.at[d],
                    self.lined.at[d],
                    self.sems.at[2, d],
                    self.sems.at[3, d],
                    to * PAIR + side,
                )
            )

    def total(self):
        self.pairs[0].wait()
        me = lax.axis_index("seq")
        total = self.part[me].astype(jnp.float32) + self.paired[0].astype(jnp.float32)
        for d, copy in zip(range(1, self.lines), self.sent):
            copy.wait()
            total = total + self.lined[d].astype(jnp.float32)
        return total


class Reduce(Scatter):
    def __init__(self, lines, part, paired, middle, lined, sems, mine, gathered, crossed):
        super().__init__(lines, part, paired, middle, lined, sems)
        self.mine, self.gathered, self.crossed = mine, gathered, crossed

    def gather(self):
        self.mine[...] = rounded(self.total())
        self.out = []
        for d in range(1, self.lines):
            self.out.append(
                remote(
                    self.mine,
                    self.gathered.at[d],
                    self.sems.at[4, d],
                    self.sems.at[5, d],
                    line_peer(self.lines, d),
                )
            )
        self.across = [
            remote(
                self.mine, self.crossed.at[0], self.sems.at[6, 0], self.sems.at[7, 0], partner()
            )
        ]

    def relay(self):
        for d in range(1, self.lines):
            self.out[d - 1].wait()
            self.across.append(
                remote(
                    self.gathered.at[d],
                    self.crossed.at[d],
                    self.sems.at[6, d],
                    self.sems.at[7, d],
                    partner(),
                )
            )

    def finish(self, put):
        lines = self.lines
        line, side = place()
        rows = self.mine.shape[0]

        def place_block(owner, block):
            put(pl.ds(pl.multiple_of(owner * rows, rows), rows), block.astype(jnp.float32))

        place_block(line * PAIR + side, self.mine[...])
        for d in range(1, lines):
            place_block(lax.rem(line - d + lines, lines) * PAIR + side, self.gathered[d])
        for d in range(lines):
            self.across[d].wait()
            place_block(lax.rem(line - d + lines, lines) * PAIR + (1 - side), self.crossed[d])


def squared(parts, dot):
    along = 0 if dot is times_transpose else 1
    both = dot(parts[0], jnp.concatenate(parts, axis=along))
    wide = both.shape[1] // 2
    return both[:, :wide] + (both[:, wide:] + both[:, wide:].T)


def ns_forward(s):
    each = range(COUNT)
    for m in each:
        matrix = s.totals[m]
        s.current[m] = matrix / (jnp.sqrt(jnp.sum(matrix * matrix)) + EPS)

    def keep(k, m, x, gram, poly):
        s.xs[k, m], s.grams[k, m], s.polys[k, m] = x, gram, poly

    def single(k, carry):
        xs = [rounded(s.current[m]) for m in each]
        grams = [times_transpose(x, x) for x in xs]
        grams_r = [rounded(gram) for gram in grams]
        polys = [rounded(C3 * g + C5 * product(r, r)) for g, r in zip(grams, grams_r)]
        for m in each:
            keep(k, m, xs[m], grams_r[m], polys[m])
            s.current[m] = C1 * s.current[m] + product(polys[m], xs[m])
        return carry

    def precise(k, carry):
        xs = [split(s.current[m]) for m in each]
        grams = [squared(x, times_transpose) for x in xs]
        parts = [split(gram) for gram in grams]
        polys = [split(C3 * g + C5 * squared(p, product)) for g, p in zip(grams, parts)]
        for m in each:
            keep(k, m, xs[m][0], parts[m][0], polys[m][0])
            tall = product(jnp.concatenate(polys[m], axis=0), xs[m][0])
            rows = tall.shape[0] // 2
            s.current[m] = (
                C1 * s.current[m]
                + (tall[:rows] + tall[rows:])
                + product(polys[m][0], xs[m][1])
            )
        return carry

    lax.fori_loop(0, NS_SINGLE, single, 0)
    lax.fori_loop(NS_SINGLE, NS_STEPS, precise, 0)


def ns_backward(s, first, last):
    each = range(COUNT)

    def step(i, carry):
        k = NS_STEPS - 1 - i
        grads = [rounded(s.current[m]) for m in each]
        dpolys = [times_transpose(grads[m], s.xs[k, m]) for m in each]
        syms = [dpoly + dpoly.T for dpoly in dpolys]
        twists = [product(rounded(syms[m]), s.grams[k, m]) for m in each]
        weights = [rounded(C3 * sym + C5 * (t + t.T)) for sym, t in zip(syms, twists)]
        for m in each:
            s.current[m] = C1 * s.current[m] + product(
                jnp.concatenate([s.polys[k, m], weights[m]], axis=1),
                jnp.concatenate([grads[m], s.xs[k, m]], axis=0),
            )
        return carry

    lax.fori_loop(first, last, step, 0)


def ns_finish(s):
    each = range(COUNT)
    results = []
    for m in each:
        matrix, grad = s.totals[m], s.current[m]
        norm = jnp.sqrt(jnp.sum(matrix * matrix))
        shifted = norm + EPS
        dot_all = jnp.sum(grad * matrix)
        results.append(
            rounded(grad / shifted - matrix * (dot_all / (norm * shifted * shifted)))
        )
    return results


OPERANDS = (
    "inputs", "rates", "proj_query", "proj_key", "proj_value", "proj_output",
    "fast_in", "fast_up", "fast_out", "cotangent",
)
RESULTS = (
    "back_hbm", "rate_hbm", "in_hbm", "up_hbm", "out_hbm",
    "query_hbm", "key_hbm", "value_hbm", "output_hbm",
)


def scratch_of(n, tokens, width, h, f):
    lines = n // PAIR
    rows, wide_rows = h // n, width // n
    bf16, f32 = jnp.bfloat16, jnp.float32
    tile = math.gcd(tokens, 256)
    v = pltpu.VMEM
    return dict(
        x=v((tokens, width), bf16),
        cot=v((tokens, width), bf16),
        x_t=v((width, tokens), bf16),
        cot_t=v((width, tokens), bf16),
        wall=v((width, 3 * h), bf16),
        wo=v((h, width), bf16),
        rates_in=v((tokens // LANES, LANES), f32),
        rate_cols=v((tokens, LANES), f32),
        fin=v((h, f), f32),
        fup=v((h, f), f32),
        fout_t=v((h, f), f32),
        b4=v((h, 4 * f), bf16),
        bow=v((h, 2 * f), bf16),
        nw=v((h, 2 * f), bf16),
        no_t=v((h, f), bf16),
        key=v((tokens, h), bf16),
        value=v((tokens, h), bf16),
        scaled=v((tokens, h), bf16),
        key_t=v((h, tokens), bf16),
        scaled_t=v((h, tokens), bf16),
        query=v((tokens, h), bf16),
        back_out=v((tokens, h), bf16),
        pre=v((tokens, 2 * f), f32),
        ups=v((tokens, f), f32),
        work=v((tile, 3 * f), f32),
        hb=v((tokens, 2 * f), bf16),
        g4=v((tokens, 4 * f), bf16),
        hq=v((tokens, f), bf16),
        bpr=v((tokens, 2 * f), bf16),
        **({} if 3 * h == width else dict(grads=v((tokens, 3 * h), bf16))),
        rate_out=v((tokens // LANES, LANES), f32),
        xs=v((NS_STEPS, COUNT, h, f), bf16),
        grams=v((NS_STEPS, COUNT, h, h), bf16),
        polys=v((NS_STEPS, COUNT, h, h), bf16),
        current=v((COUNT, h, f), f32),
        totals=v((COUNT, h, f), f32),
        adjoint=v((COUNT, h, f), bf16),
        gout=v((f, h), f32),
        row_sums=v((GROUPS, wide_rows, h), f32),
        part=v((COUNT, n, rows, f), bf16),
        middle=v((COUNT, lines, rows, f), bf16),
        mine=v((COUNT, rows, f), bf16),
        paired=v((ROUNDS, COUNT, lines, rows, f), bf16),
        lined=v((ROUNDS, COUNT, lines, rows, f), bf16),
        gathered=v((ROUNDS, COUNT, lines, rows, f), bf16),
        crossed=v((ROUNDS, COUNT, lines, rows, f), bf16),
        sems=pltpu.SemaphoreType.DMA((ROUNDS, COUNT, 8, lines)),
        row_part=v((GROUPS, n, wide_rows, h), bf16),
        row_paired=v((GROUPS, lines, wide_rows, h), bf16),
        row_middle=v((GROUPS, lines, wide_rows, h), bf16),
        row_lined=v((GROUPS, lines, wide_rows, h), bf16),
        row_sems=pltpu.SemaphoreType.DMA((GROUPS, 4, lines)),
        load_sems=pltpu.SemaphoreType.DMA((8,)),
        x_sems=pltpu.SemaphoreType.DMA((tokens // tile,)),
        cot_sems=pltpu.SemaphoreType.DMA((tokens // tile,)),
        store_sems=pltpu.SemaphoreType.DMA((len(RESULTS),)),
    )


def kernel(n, names, *refs):
    s = SimpleNamespace(**dict(zip(names, refs)))
    lines = n // PAIR
    tokens, width = s.x.shape
    h, f = s.fin.shape
    if 3 * h == width:
        s.grads = s.x
    tile = math.gcd(tokens, 256)
    tiles = tokens // tile
    sub = math.gcd(tile, 32)
    half = math.gcd(f, 256)
    f32 = jnp.float32

    def rows_at(i, size=tile):
        return pl.ds(pl.multiple_of(i * size, size), size)

    def each_tile(step, first=0, last=tiles):
        for i in range(first, last):
            step(i, pl.ds(i * tile, tile))

    def over_tiles(step, first=0, last=tiles):
        def body(i, carry):
            step(i, rows_at(i))
            return carry

        lax.fori_loop(first, last, body, 0)

    def rows_from(i, j):
        start = i * tile + j * sub
        return pl.ds(start if isinstance(start, int) else pl.multiple_of(start, sub), sub)

    def over_subs(step):
        for i in range(tile // sub):
            for j in range(f // half):
                step(i, j * half)

    def load(src, dst, sem):
        copy = pltpu.make_async_copy(src, dst, sem)
        copy.start()
        return copy

    def x_copy(i, at):
        return pltpu.make_async_copy(s.inputs.at[at], s.x.at[at], s.x_sems.at[i])

    def cot_copy(i, at):
        return pltpu.make_async_copy(s.cotangent.at[at], s.cot.at[at], s.cot_sems.at[i])

    reduces = [
        [
            Reduce(
                lines, s.part.at[c], s.paired.at[r, c], s.middle.at[c], s.lined.at[r, c],
                s.sems.at[r, c], s.mine.at[c], s.gathered.at[r, c], s.crossed.at[r, c],
            )
            for c in range(COUNT)
        ]
        for r in range(ROUNDS)
    ]
    scatters = [
        Scatter(
            lines, s.row_part.at[g], s.row_paired.at[g], s.row_middle.at[g], s.row_lined.at[g],
            s.row_sems.at[g],
        )
        for g in range(GROUPS)
    ]

    greet(lines)
    x_copy(0, pl.ds(0, tile)).start()
    loads = [
        load(s.proj_key, s.wall.at[:, h : 2 * h], s.load_sems.at[0]),
        load(s.proj_value, s.wall.at[:, 2 * h :], s.load_sems.at[1]),
        load(s.rates, s.rates_in, s.load_sems.at[2]),
        load(s.fast_in, s.fin, s.load_sems.at[3]),
        load(s.fast_up, s.fup, s.load_sems.at[4]),
        load(s.fast_out, s.gout, s.load_sems.at[5]),
    ]
    for i in range(1, tiles):
        x_copy(i, pl.ds(i * tile, tile)).start()
    loads += [
        load(s.proj_query, s.wall.at[:, :h], s.load_sems.at[6]),
        load(s.proj_output, s.wo, s.load_sems.at[7]),
    ]
    for i in range(tiles):
        cot_copy(i, pl.ds(i * tile, tile)).start()

    for copy in loads[:6]:
        copy.wait()
    s.b4[:, 2 * f : 3 * f] = rounded(s.fin[...])
    s.b4[:, 3 * f :] = rounded(s.fup[...])
    s.fout_t[...] = s.gout[...].T
    s.bow[:, f:] = rounded(s.fout_t[...])
    for i in range(tokens // LANES):
        s.rate_cols[i * LANES : (i + 1) * LANES, :] = jnp.broadcast_to(
            s.rates_in[i : i + 1, :], (LANES, LANES)
        ).T

    def rate_of(at, wide):
        return jnp.concatenate([s.rate_cols[at, :]] * (wide // LANES), axis=1)

    def update(i, at):
        x_copy(i, at).wait()
        both = product(s.x[at, :], s.wall[:, h:])
        key = rounded(both[:, :h])
        value = rounded(both[:, h:])
        scaled = rounded(rate_of(at, h) * value.astype(f32))
        s.key[at, :], s.value[at, :], s.scaled[at, :] = key, value, scaled
        s.pre[at, :] = product(key, s.b4[:, 2 * f :])
        s.ups[at, :] = product(scaled, s.bow[:, f:])
        s.key_t[:, at] = key.T
        s.scaled_t[:, at] = scaled.T

        def point(j, col):
            to = rows_from(i, j)
            pre_in, pre_up = s.pre[to, col : col + half], s.pre[to, f + col : f + col + half]
            up = s.ups[to, col : col + half]
            _, activation, slope = sigmoid_slope(pre_in)
            s.hb[to, col : col + half] = rounded(activation * pre_up)
            s.g4[to, col : col + half] = rounded(up * pre_up * slope)
            s.g4[to, f + col : f + col + half] = rounded(up * activation)

        over_subs(point)

    each_tile(update)
    for copy in loads[6:]:
        copy.wait()

    def project(i, at):
        s.query[at, :] = rounded(product(s.x[at, :], s.wall[:, :h]))
        cot_copy(i, at).wait()
        s.back_out[at, :] = rounded(times_transpose(s.cot[at, :], s.wo[...]))

    def turn(i, at):
        s.x_t[:, at] = s.x[at, :].T
        s.cot_t[:, at] = s.cot[at, :].T

    second = lax.rem(lax.axis_index("batch"), 2) == 0
    first = jnp.logical_not(second)

    @pl.when(second)
    def _():
        over_tiles(project)
        over_tiles(turn)

    greeted(lines)
    now = reduces[0]
    now[0].fill(product(s.key_t[...], s.g4[:, :f]))
    now[0].start()
    now[1].fill(product(s.key_t[...], s.g4[:, f : 2 * f]))
    now[1].start()
    now[2].fill(product(s.scaled_t[...], s.hb[:, :f]))
    now[2].start()

    def total_put(m):
        def put(at, block):
            s.totals[m, at, :] = block

        return put

    @pl.when(first)
    def _():
        over_tiles(project, 0, tiles // 2)

    now[0].forward()

    @pl.when(first)
    def _():
        over_tiles(project, tiles // 2, tiles)

    now[1].forward()
    now[0].gather()

    @pl.when(first)
    def _():
        over_tiles(turn)

    now[2].forward()
    now[1].gather()
    now[0].relay()
    now[2].gather()
    now[1].relay()
    now[2].relay()
    for m in range(COUNT):
        now[m].finish(total_put(m))
    ns_forward(s)
    s.nw[:, :f] = rounded(s.fin[...] + s.current[0])
    s.nw[:, f:] = rounded(s.fup[...] + s.current[1])
    s.no_t[...] = rounded(s.fout_t[...] + s.current[2])

    def query(i, at):
        s.work[:, : 2 * f] = product(s.query[at, :], s.nw[...])
        s.work[:, 2 * f :] = product(s.back_out[at, :], s.no_t[...])

        def point(j, col):
            here = pl.ds(j * sub, sub)
            to = rows_from(i, j)
            pre_p = s.work[here, col : col + half]
            pre_r = s.work[here, f + col : f + col + half]
            back = s.work[here, 2 * f + col : 2 * f + col + half]
            _, activation, slope = sigmoid_slope(pre_p)
            s.hq[to, col : col + half] = rounded(activation * pre_r)
            s.bpr[to, col : col + half] = rounded(back * pre_r * slope)
            s.bpr[to, f + col : f + col + half] = rounded(back * activation)

        over_subs(point)

    over_tiles(query)
    now = reduces[1]
    now[2].fill(token_sum(s.back_out[...], s.hq[...]))
    now[2].start()
    query_sums = token_sum(s.query[...], s.bpr[...])
    now[0].fill(query_sums)
    now[0].start()
    now[1].fill(query_sums, f)
    now[1].start()

    def adjoint_put(m):
        def put(at, block):
            s.adjoint[m, at, :] = rounded(block)

        return put

    def query_back(i, at):
        s.grads[at, :h] = rounded(times_transpose(s.bpr[at, :], s.nw[...]))
        s.grads[at, h : 2 * h] = rounded(times_transpose(s.hq[at, :], s.no_t[...]))

    now[2].forward()
    over_tiles(query_back)
    now[0].forward()
    now[2].gather()
    scatters[0].fill(product(s.x_t[...], s.grads[:, :h]))
    now[1].forward()
    now[0].gather()
    now[2].relay()
    scatters[1].fill(product(s.cot_t[...], s.grads[:, h : 2 * h]))
    now[1].gather()
    now[0].relay()
    now[1].relay()
    scatters[0].start()
    scatters[1].start()
    for m in (2, 0, 1):
        now[m].finish(adjoint_put(m))
    for m in range(COUNT):
        s.current[m] = s.adjoint[m].astype(f32)
    ns_backward(s, 0, NS_STEPS - 1)
    scatters[0].forward()
    ns_backward(s, NS_STEPS - 1, NS_STEPS)
    s.b4[:, :f], s.b4[:, f : 2 * f], s.bow[:, :f] = ns_finish(s)

    def update_back(i, at):
        s.work[:, : 2 * f] = product(s.key[at, :], s.b4[:, : 2 * f])
        s.work[:, 2 * f :] = product(s.scaled[at, :], s.bow[:, :f])

        def point(j, col):
            here = pl.ds(j * sub, sub)
            to = rows_from(i, j)
            press_in = s.work[here, col : col + half]
            press_up = s.work[here, f + col : f + col + half]
            back_hid = s.work[here, 2 * f + col : 2 * f + col + half]
            pre_in, pre_up = s.pre[to, col : col + half], s.pre[to, f + col : f + col + half]
            up = s.ups[to, col : col + half]
            sigma, activation, slope = sigmoid_slope(pre_in)
            rest = 1.0 - sigma
            curvature = sigma * rest * (2.0 + pre_in * (rest - sigma))
            press_slope = press_in * slope
            s.hb[to, f + col : f + col + half] = rounded(press_slope * pre_up + press_up * activation)
            s.g4[to, 3 * f + col : 3 * f + col + half] = rounded(
                press_slope * up + back_hid * activation
            )
            s.g4[to, 2 * f + col : 2 * f + col + half] = rounded(
                press_in * up * pre_up * curvature + (press_up * up + back_hid * pre_up) * slope
            )

        over_subs(point)

    over_tiles(update_back, 0, tiles // 2)
    scatters[1].forward()
    over_tiles(update_back, tiles // 2, tiles)
    now = reduces[2]
    now[2].fill(product(s.scaled_t[...], s.hb[:, f:]))
    now[2].start()
    now[0].fill(product(s.key_t[...], s.g4[:, 2 * f : 3 * f]))
    now[0].start()
    now[1].fill(product(s.key_t[...], s.g4[:, 3 * f :]))
    now[1].start()

    def token_back(i, at):
        back_scaled = times_transpose(s.hb[at, :], s.bow[...])
        weighed = back_scaled * s.value[at, :].astype(f32)
        for t in range(tile // LANES):
            block = weighed[t * LANES : (t + 1) * LANES, :]
            folded = block[:, :LANES]
            for c in range(1, h // LANES):
                folded = folded + block[:, c * LANES : (c + 1) * LANES]
            s.rate_out[pl.ds(i * (tile // LANES) + t, 1), :] = jnp.sum(
                folded.T, axis=0, keepdims=True
            )
        s.grads[at, 2 * h :] = rounded(rate_of(at, h) * back_scaled)
        s.grads[at, h : 2 * h] = rounded(times_transpose(s.g4[at, :], s.b4[...]))

    over_tiles(token_back, 0, tiles // 2)
    now[2].forward()
    over_tiles(token_back, tiles // 2, tiles)
    stores = [
        load(s.rate_out, s.rate_hbm, s.store_sems.at[1]),
    ]
    now[0].forward()
    now[2].gather()
    key_value = product(s.x_t[...], s.grads[:, h:])
    scatters[2].fill(key_value)
    scatters[2].start()
    scatters[3].fill(key_value, h)
    scatters[3].start()
    now[1].forward()
    now[0].gather()

    def inputs_back(i, at):
        s.cot[at, :] = rounded(times_transpose(s.grads[at, :], s.wall[...]))

    over_tiles(inputs_back)
    stores.append(load(s.cot, s.back_hbm, s.store_sems.at[0]))
    now[2].relay()
    scatters[2].forward()
    now[1].gather()
    now[0].relay()
    scatters[3].forward()
    now[1].relay()

    def sum_put(m):
        def put(at, block):
            s.totals[m, at, :] = s.adjoint[m, at, :].astype(f32) + block

        return put

    for g, (to, sem) in enumerate(((s.query_hbm, 5), (s.output_hbm, 8))):
        s.row_sums[g] = scatters[g].total()
        stores.append(load(s.row_sums.at[g], to, s.store_sems.at[sem]))
    now[2].finish(sum_put(2))
    s.gout[...] = s.totals[2].T
    stores.append(load(s.gout, s.out_hbm, s.store_sems.at[4]))
    now[0].finish(sum_put(0))
    stores.append(load(s.totals.at[0], s.in_hbm, s.store_sems.at[2]))
    for g, (to, sem) in ((2, (s.key_hbm, 6)), (3, (s.value_hbm, 7))):
        s.row_sums[g] = scatters[g].total()
        stores.append(load(s.row_sums.at[g], to, s.store_sems.at[sem]))
    now[1].finish(sum_put(1))
    stores.append(load(s.totals.at[1], s.up_hbm, s.store_sems.at[3]))
    for copy in stores:
        copy.wait()


def pieces_of(shape, kind):
    size = math.prod(shape) * jnp.dtype(kind).itemsize
    count = max(1, min(size // PIECE, shape[0] // LANES))
    while shape[0] % (16 * count) and count > 1:
        count -= 1
    step = shape[0] // count
    return [pl.ds(i * step, step) for i in range(count)]


def copy_kernel(count, *refs):
    sources, targets, holds = (refs[i * count : (i + 1) * count] for i in range(3))
    sems = refs[-1]
    moves = [
        (src.at[at], hold.at[at], dst.at[at])
        for src, dst, hold in zip(sources, targets, holds)
        for at in pieces_of(src.shape, src.dtype)
    ]
    loads = [
        pltpu.make_async_copy(src, hold, sems.at[0, i])
        for i, (src, hold, _) in enumerate(moves)
    ]
    stores = [
        pltpu.make_async_copy(hold, dst, sems.at[1, i])
        for i, (_, hold, dst) in enumerate(moves)
    ]
    for load in loads:
        load.start()
    for load, store in zip(loads, stores):
        load.wait()
        store.start()
    for store in stores:
        store.wait()


def body(n, *operands):
    inputs, rates, fast_in = operands[0], operands[1], operands[6]
    tokens, width = inputs.shape
    h, f = fast_in.shape
    wide_rows = width // n
    bf16, f32 = jnp.bfloat16, jnp.float32
    outs = [
        ((tokens, width), bf16),
        ((tokens // LANES, LANES), f32),
        ((h, f), f32),
        ((h, f), f32),
        ((f, h), f32),
        ((wide_rows, h), f32),
        ((wide_rows, h), f32),
        ((wide_rows, h), f32),
        ((wide_rows, h), f32),
    ]
    scratch = scratch_of(n, tokens, width, h, f)
    anywhere = pl.BlockSpec(memory_space=pl.ANY)
    operands = list(operands)
    operands[1] = rates.reshape(tokens // LANES, LANES)
    results = pl.pallas_call(
        functools.partial(kernel, n, OPERANDS + RESULTS + tuple(scratch)),
        out_shape=[jax.ShapeDtypeStruct(shape, kind) for shape, kind in outs],
        in_specs=[anywhere] * len(operands),
        out_specs=[anywhere] * len(outs),
        scratch_shapes=list(scratch.values()),
        compiler_params=pltpu.CompilerParams(
            collective_id=0, has_side_effects=True, vmem_limit_bytes=VMEM_LIMIT
        ),
    )(*operands)

    moves = sum(len(pieces_of(shape, kind)) for shape, kind in outs)
    return pl.pallas_call(
        functools.partial(copy_kernel, len(outs)),
        out_shape=[jax.ShapeDtypeStruct(shape, kind) for shape, kind in outs],
        in_specs=[anywhere] * len(outs),
        out_specs=[anywhere] * len(outs),
        scratch_shapes=[pltpu.VMEM(shape, kind) for shape, kind in outs]
        + [pltpu.SemaphoreType.DMA((2, moves))],
    )(*results)


def solution(mesh):
    n = mesh.shape["seq"]

    def step(*operands):
        outs = body(n, *operands)
        return (outs[0], outs[1].reshape(-1)) + tuple(outs[2:8]) + (outs[8].T,)

    in_specs = (
        P(("batch", "seq"), None),
        P(("batch", "seq")),
        P(),
        P(),
        P(),
        P(),
        P(),
        P(),
        P(),
        P(("batch", "seq"), None),
    )
    out_specs = (
        P(("batch", "seq"), None),
        P(("batch", "seq")),
        P("batch", None),
        P("batch", None),
        P("batch", None),
        P("seq", "batch"),
        P("seq", "batch"),
        P("seq", "batch"),
        P("batch", "seq"),
    )
    return jax.shard_map(
        step, mesh=mesh, in_specs=in_specs, out_specs=out_specs, check_vma=False
    )
```

```python
import functools
import math
from types import SimpleNamespace

import jax
import jax.numpy as jnp
from jax import lax
from jax.experimental import pallas as pl
from jax.experimental.pallas import tpu as pltpu
from jax.sharding import PartitionSpec as P

NS_STEPS = 5
NS_SINGLE = 2
C1, C3, C5 = 3.4445, -4.775, 2.0315
EPS = 1e-07
MESH = pl.DeviceIdType.MESH
VMEM_LIMIT = 66_000_000
PAIR = 2
COUNT = 3
LANES = 128
ROUNDS = 3
GROUPS = 4
PIECE = 384 * 1024


def rounded(value):
    return value.astype(jnp.bfloat16)


def product(left, right):
    return jnp.dot(left, right, preferred_element_type=jnp.float32)


def token_sum(left, right):
    return lax.dot_general(
        left, right, (((0,), (0,)), ((), ())), preferred_element_type=jnp.float32
    )


def times_transpose(left, right):
    return lax.dot_general(
        left, right, (((1,), (1,)), ((), ())), preferred_element_type=jnp.float32
    )


def sigmoid_slope(pre_act):
    sigma = jax.nn.sigmoid(pre_act)
    return sigma, pre_act * sigma, sigma * (1.0 + pre_act * (1.0 - sigma))


def split(value):
    high = rounded(value)
    return (high, rounded(value - high.astype(jnp.float32)))


def place():
    me = lax.axis_index("seq")
    return me // PAIR, me % PAIR


def remote(src, dst, send, recv, device):
    copy = pltpu.make_async_remote_copy(
        src_ref=src,
        dst_ref=dst,
        send_sem=send,
        recv_sem=recv,
        device_id={"seq": device},
        device_id_type=MESH,
    )
    copy.start()
    return copy


def line_peer(lines, d):
    line, side = place()
    return lax.rem(line + d, lines) * PAIR + side


def partner():
    line, side = place()
    return line * PAIR + (1 - side)


def greet(lines):
    barrier = pltpu.get_barrier_semaphore()
    for peer in [partner()] + [line_peer(lines, d) for d in range(1, lines)]:
        pl.semaphore_signal(barrier, inc=1, device_id={"seq": peer}, device_id_type=MESH)


def greeted(lines):
    pl.semaphore_wait(pltpu.get_barrier_semaphore(), lines)


class Scatter:
    def __init__(self, lines, part, paired, middle, lined, sems):
        self.lines = lines
        self.part, self.paired, self.middle, self.lined = part, paired, middle, lined
        self.sems = sems

    def fill(self, total, at=0):
        n, rows, wide = self.part.shape
        for j in range(n):
            self.part[j] = rounded(total[j * rows : (j + 1) * rows, at : at + wide])

    def start(self):
        lines = self.lines
        line, side = place()
        self.pairs = {}
        for d in list(range(1, lines)) + [0]:
            to = lax.rem(line + d, lines)
            self.pairs[d] = remote(
                self.part.at[to * PAIR + (1 - side)],
                self.paired.at[d],
                self.sems.at[0, d],
                self.sems.at[1, d],
                partner(),
            )

    def forward(self):
        lines = self.lines
        line, side = place()
        self.sent = []
        for d in range(1, lines):
            to = lax.rem(line + d, lines)
            self.pairs[d].wait()
            self.middle[d] = rounded(
                self.part[to * PAIR + side].astype(jnp.float32)
                + self.paired[d].astype(jnp.float32)
            )
            self.sent.append(
                remote(
                    self.middle.at[d],
                    self.lined.at[d],
                    self.sems.at[2, d],
                    self.sems.at[3, d],
                    to * PAIR + side,
                )
            )

    def total(self):
        self.pairs[0].wait()
        me = lax.axis_index("seq")
        total = self.part[me].astype(jnp.float32) + self.paired[0].astype(jnp.float32)
        for d, copy in zip(range(1, self.lines), self.sent):
            copy.wait()
            total = total + self.lined[d].astype(jnp.float32)
        return total


class Reduce(Scatter):
    def __init__(self, lines, part, paired, middle, lined, sems, mine, gathered, crossed):
        super().__init__(lines, part, paired, middle, lined, sems)
        self.mine, self.gathered, self.crossed = mine, gathered, crossed

    def gather(self):
        self.mine[...] = rounded(self.total())
        self.out = []
        for d in range(1, self.lines):
            self.out.append(
                remote(
                    self.mine,
                    self.gathered.at[d],
                    self.sems.at[4, d],
                    self.sems.at[5, d],
                    line_peer(self.lines, d),
                )
            )
        self.across = [
            remote(
                self.mine, self.crossed.at[0], self.sems.at[6, 0], self.sems.at[7, 0], partner()
            )
        ]

    def relay(self):
        for d in range(1, self.lines):
            self.out[d - 1].wait()
            self.across.append(
                remote(
                    self.gathered.at[d],
                    self.crossed.at[d],
                    self.sems.at[6, d],
                    self.sems.at[7, d],
                    partner(),
                )
            )

    def finish(self, put):
        lines = self.lines
        line, side = place()
        rows = self.mine.shape[0]

        def place_block(owner, block):
            put(pl.ds(pl.multiple_of(owner * rows, rows), rows), block.astype(jnp.float32))

        place_block(line * PAIR + side, self.mine[...])
        for d in range(1, lines):
            place_block(lax.rem(line - d + lines, lines) * PAIR + side, self.gathered[d])
        for d in range(lines):
            self.across[d].wait()
            place_block(lax.rem(line - d + lines, lines) * PAIR + (1 - side), self.crossed[d])


def squared(parts, dot):
    along = 0 if dot is times_transpose else 1
    both = dot(parts[0], jnp.concatenate(parts, axis=along))
    wide = both.shape[1] // 2
    return both[:, :wide] + (both[:, wide:] + both[:, wide:].T)


def ns_forward(s):
    each = range(COUNT)
    for m in each:
        matrix = s.totals[m]
        s.current[m] = matrix / (jnp.sqrt(jnp.sum(matrix * matrix)) + EPS)

    def keep(k, m, x, gram, poly):
        s.xs[k, m], s.grams[k, m], s.polys[k, m] = x, gram, poly

    def single(k, carry):
        xs = [rounded(s.current[m]) for m in each]
        grams = [times_transpose(x, x) for x in xs]
        grams_r = [rounded(gram) for gram in grams]
        polys = [rounded(C3 * g + C5 * product(r, r)) for g, r in zip(grams, grams_r)]
        for m in each:
            keep(k, m, xs[m], grams_r[m], polys[m])
            s.current[m] = C1 * s.current[m] + product(polys[m], xs[m])
        return carry

    def precise(k, carry):
        xs = [split(s.current[m]) for m in each]
        grams = [squared(x, times_transpose) for x in xs]
        parts = [split(gram) for gram in grams]
        polys = [split(C3 * g + C5 * squared(p, product)) for g, p in zip(grams, parts)]
        for m in each:
            keep(k, m, xs[m][0], parts[m][0], polys[m][0])
            tall = product(jnp.concatenate(polys[m], axis=0), xs[m][0])
            rows = tall.shape[0] // 2
            s.current[m] = (
                C1 * s.current[m]
                + (tall[:rows] + tall[rows:])
                + product(polys[m][0], xs[m][1])
            )
        return carry

    lax.fori_loop(0, NS_SINGLE, single, 0)
    lax.fori_loop(NS_SINGLE, NS_STEPS, precise, 0)


def ns_backward(s, first, last):
    each = range(COUNT)

    def step(i, carry):
        k = NS_STEPS - 1 - i
        grads = [rounded(s.current[m]) for m in each]
        dpolys = [times_transpose(grads[m], s.xs[k, m]) for m in each]
        syms = [dpoly + dpoly.T for dpoly in dpolys]
        twists = [product(rounded(syms[m]), s.grams[k, m]) for m in each]
        weights = [rounded(C3 * sym + C5 * (t + t.T)) for sym, t in zip(syms, twists)]
        for m in each:
            s.current[m] = C1 * s.current[m] + product(
                jnp.concatenate([s.polys[k, m], weights[m]], axis=1),
                jnp.concatenate([grads[m], s.xs[k, m]], axis=0),
            )
        return carry

    lax.fori_loop(first, last, step, 0)


def ns_finish(s):
    each = range(COUNT)
    results = []
    for m in each:
        matrix, grad = s.totals[m], s.current[m]
        norm = jnp.sqrt(jnp.sum(matrix * matrix))
        shifted = norm + EPS
        dot_all = jnp.sum(grad * matrix)
        results.append(
            rounded(grad / shifted - matrix * (dot_all / (norm * shifted * shifted)))
        )
    return results


OPERANDS = (
    "inputs", "rates", "proj_query", "proj_key", "proj_value", "proj_output",
    "fast_in", "fast_up", "fast_out", "cotangent",
)
RESULTS = (
    "back_hbm", "rate_hbm", "in_hbm", "up_hbm", "out_hbm",
    "query_hbm", "key_hbm", "value_hbm", "output_hbm",
)


def scratch_of(n, tokens, width, h, f):
    lines = n // PAIR
    rows, wide_rows = h // n, width // n
    bf16, f32 = jnp.bfloat16, jnp.float32
    tile = math.gcd(tokens, 256)
    v = pltpu.VMEM
    return dict(
        x=v((tokens, width), bf16),
        cot=v((tokens, width), bf16),
        x_t=v((width, tokens), bf16),
        cot_t=v((width, tokens), bf16),
        wall=v((width, 3 * h), bf16),
        wo=v((h, width), bf16),
        rates_in=v((tokens // LANES, LANES), f32),
        rate_cols=v((tokens, LANES), f32),
        fin=v((h, f), f32),
        fup=v((h, f), f32),
        fout_t=v((h, f), f32),
        b4=v((h, 4 * f), bf16),
        bow=v((h, 2 * f), bf16),
        nw=v((h, 2 * f), bf16),
        no_t=v((h, f), bf16),
        key=v((tokens, h), bf16),
        value=v((tokens, h), bf16),
        scaled=v((tokens, h), bf16),
        key_t=v((h, tokens), bf16),
        scaled_t=v((h, tokens), bf16),
        query=v((tokens, h), bf16),
        back_out=v((tokens, h), bf16),
        pre=v((tokens, 2 * f), f32),
        ups=v((tokens, f), f32),
        work=v((tile, 3 * f), f32),
        hb=v((tokens, 2 * f), bf16),
        g4=v((tokens, 4 * f), bf16),
        hq=v((tokens, f), bf16),
        bpr=v((tokens, 2 * f), bf16),
        **({} if 3 * h == width else dict(grads=v((tokens, 3 * h), bf16))),
        rate_out=v((tokens // LANES, LANES), f32),
        xs=v((NS_STEPS, COUNT, h, f), bf16),
        grams=v((NS_STEPS, COUNT, h, h), bf16),
        polys=v((NS_STEPS, COUNT, h, h), bf16),
        current=v((COUNT, h, f), f32),
        totals=v((COUNT, h, f), f32),
        adjoint=v((COUNT, h, f), bf16),
        gout=v((f, h), f32),
        row_sums=v((GROUPS, wide_rows, h), f32),
        part=v((COUNT, n, rows, f), bf16),
        middle=v((COUNT, lines, rows, f), bf16),
        mine=v((COUNT, rows, f), bf16),
        paired=v((ROUNDS, COUNT, lines, rows, f), bf16),
        lined=v((ROUNDS, COUNT, lines, rows, f), bf16),
        gathered=v((ROUNDS, COUNT, lines, rows, f), bf16),
        crossed=v((ROUNDS, COUNT, lines, rows, f), bf16),
        sems=pltpu.SemaphoreType.DMA((ROUNDS, COUNT, 8, lines)),
        row_part=v((GROUPS, n, wide_rows, h), bf16),
        row_paired=v((GROUPS, lines, wide_rows, h), bf16),
        row_middle=v((GROUPS, lines, wide_rows, h), bf16),
        row_lined=v((GROUPS, lines, wide_rows, h), bf16),
        row_sems=pltpu.SemaphoreType.DMA((GROUPS, 4, lines)),
        load_sems=pltpu.SemaphoreType.DMA((8,)),
        x_sems=pltpu.SemaphoreType.DMA((tokens // tile,)),
        cot_sems=pltpu.SemaphoreType.DMA((tokens // tile,)),
        store_sems=pltpu.SemaphoreType.DMA((len(RESULTS),)),
    )


def kernel(n, names, *refs):
    s = SimpleNamespace(**dict(zip(names, refs)))
    lines = n // PAIR
    tokens, width = s.x.shape
    h, f = s.fin.shape
    if 3 * h == width:
        s.grads = s.x
    tile = math.gcd(tokens, 256)
    tiles = tokens // tile
    sub = math.gcd(tile, 32)
    half = math.gcd(f, 256)
    f32 = jnp.float32

    def rows_at(i, size=tile):
        return pl.ds(pl.multiple_of(i * size, size), size)

    def each_tile(step, first=0, last=tiles):
        for i in range(first, last):
            step(i, pl.ds(i * tile, tile))

    def over_tiles(step, first=0, last=tiles):
        def body(i, carry):
            step(i, rows_at(i))
            return carry

        lax.fori_loop(first, last, body, 0)

    def rows_from(i, j):
        start = i * tile + j * sub
        return pl.ds(start if isinstance(start, int) else pl.multiple_of(start, sub), sub)

    def over_subs(step):
        for i in range(tile // sub):
            for j in range(f // half):
                step(i, j * half)

    def load(src, dst, sem):
        copy = pltpu.make_async_copy(src, dst, sem)
        copy.start()
        return copy

    def x_copy(i, at):
        return pltpu.make_async_copy(s.inputs.at[at], s.x.at[at], s.x_sems.at[i])

    def cot_copy(i, at):
        return pltpu.make_async_copy(s.cotangent.at[at], s.cot.at[at], s.cot_sems.at[i])

    reduces = [
        [
            Reduce(
                lines, s.part.at[c], s.paired.at[r, c], s.middle.at[c], s.lined.at[r, c],
                s.sems.at[r, c], s.mine.at[c], s.gathered.at[r, c], s.crossed.at[r, c],
            )
            for c in range(COUNT)
        ]
        for r in range(ROUNDS)
    ]
    scatters = [
        Scatter(
            lines, s.row_part.at[g], s.row_paired.at[g], s.row_middle.at[g], s.row_lined.at[g],
            s.row_sems.at[g],
        )
        for g in range(GROUPS)
    ]

    greet(lines)
    x_copy(0, pl.ds(0, tile)).start()
    loads = [
        load(s.proj_key, s.wall.at[:, h : 2 * h], s.load_sems.at[0]),
        load(s.proj_value, s.wall.at[:, 2 * h :], s.load_sems.at[1]),
        load(s.rates, s.rates_in, s.load_sems.at[2]),
        load(s.fast_in, s.fin, s.load_sems.at[3]),
        load(s.fast_up, s.fup, s.load_sems.at[4]),
        load(s.fast_out, s.gout, s.load_sems.at[5]),
    ]
    for i in range(1, tiles):
        x_copy(i, pl.ds(i * tile, tile)).start()
    loads += [
        load(s.proj_query, s.wall.at[:, :h], s.load_sems.at[6]),
        load(s.proj_output, s.wo, s.load_sems.at[7]),
    ]
    for i in range(tiles):
        cot_copy(i, pl.ds(i * tile, tile)).start()

    for copy in loads[:6]:
        copy.wait()
    s.b4[:, 2 * f : 3 * f] = rounded(s.fin[...])
    s.b4[:, 3 * f :] = rounded(s.fup[...])
    s.fout_t[...] = s.gout[...].T
    s.bow[:, f:] = rounded(s.fout_t[...])
    for i in range(tokens // LANES):
        s.rate_cols[i * LANES : (i + 1) * LANES, :] = jnp.broadcast_to(
            s.rates_in[i : i + 1, :], (LANES, LANES)
        ).T

    def rate_of(at, wide):
        return jnp.concatenate([s.rate_cols[at, :]] * (wide // LANES), axis=1)

    def update(i, at):
        x_copy(i, at).wait()
        both = product(s.x[at, :], s.wall[:, h:])
        key = rounded(both[:, :h])
        value = rounded(both[:, h:])
        scaled = rounded(rate_of(at, h) * value.astype(f32))
        s.key[at, :], s.value[at, :], s.scaled[at, :] = key, value, scaled
        s.pre[at, :] = product(key, s.b4[:, 2 * f :])
        s.ups[at, :] = product(scaled, s.bow[:, f:])
        s.key_t[:, at] = key.T
        s.scaled_t[:, at] = scaled.T

        def point(j, col):
            to = rows_from(i, j)
            pre_in, pre_up = s.pre[to, col : col + half], s.pre[to, f + col : f + col + half]
            up = s.ups[to, col : col + half]
            _, activation, slope = sigmoid_slope(pre_in)
            s.hb[to, col : col + half] = rounded(activation * pre_up)
            s.g4[to, col : col + half] = rounded(up * pre_up * slope)
            s.g4[to, f + col : f + col + half] = rounded(up * activation)

        over_subs(point)

    each_tile(update)
    for copy in loads[6:]:
        copy.wait()

    def project(i, at):
        s.query[at, :] = rounded(product(s.x[at, :], s.wall[:, :h]))
        cot_copy(i, at).wait()
        s.back_out[at, :] = rounded(times_transpose(s.cot[at, :], s.wo[...]))

    def turn(i, at):
        s.x_t[:, at] = s.x[at, :].T
        s.cot_t[:, at] = s.cot[at, :].T

    second = lax.rem(lax.axis_index("batch"), 2) == 0
    first = jnp.logical_not(second)

    @pl.when(second)
    def _():
        over_tiles(project)
        over_tiles(turn)

    greeted(lines)
    now = reduces[0]
    now[0].fill(product(s.key_t[...], s.g4[:, :f]))
    now[0].start()
    now[1].fill(product(s.key_t[...], s.g4[:, f : 2 * f]))
    now[1].start()
    now[2].fill(product(s.scaled_t[...], s.hb[:, :f]))
    now[2].start()

    def total_put(m):
        def put(at, block):
            s.totals[m, at, :] = block

        return put

    @pl.when(first)
    def _():
        over_tiles(project, 0, tiles // 2)

    now[0].forward()

    @pl.when(first)
    def _():
        over_tiles(project, tiles // 2, tiles)

    now[1].forward()
    now[0].gather()

    @pl.when(first)
    def _():
        over_tiles(turn)

    now[2].forward()
    now[1].gather()
    now[0].relay()
    now[2].gather()
    now[1].relay()
    now[2].relay()
    for m in range(COUNT):
        now[m].finish(total_put(m))
    ns_forward(s)
    s.nw[:, :f] = rounded(s.fin[...] + s.current[0])
    s.nw[:, f:] = rounded(s.fup[...] + s.current[1])
    s.no_t[...] = rounded(s.fout_t[...] + s.current[2])

    def query(i, at):
        s.work[:, : 2 * f] = product(s.query[at, :], s.nw[...])
        s.work[:, 2 * f :] = product(s.back_out[at, :], s.no_t[...])

        def point(j, col):
            here = pl.ds(j * sub, sub)
            to = rows_from(i, j)
            pre_p = s.work[here, col : col + half]
            pre_r = s.work[here, f + col : f + col + half]
            back = s.work[here, 2 * f + col : 2 * f + col + half]
            _, activation, slope = sigmoid_slope(pre_p)
            s.hq[to, col : col + half] = rounded(activation * pre_r)
            s.bpr[to, col : col + half] = rounded(back * pre_r * slope)
            s.bpr[to, f + col : f + col + half] = rounded(back * activation)

        over_subs(point)

    each_tile(query)
    now = reduces[1]
    now[2].fill(token_sum(s.back_out[...], s.hq[...]))
    now[2].start()
    query_sums = token_sum(s.query[...], s.bpr[...])
    now[0].fill(query_sums)
    now[0].start()
    now[1].fill(query_sums, f)
    now[1].start()

    def adjoint_put(m):
        def put(at, block):
            s.adjoint[m, at, :] = rounded(block)

        return put

    def query_back(i, at):
        s.grads[at, :h] = rounded(times_transpose(s.bpr[at, :], s.nw[...]))
        s.grads[at, h : 2 * h] = rounded(times_transpose(s.hq[at, :], s.no_t[...]))

    now[2].forward()
    over_tiles(query_back)
    now[0].forward()
    now[2].gather()
    now[1].forward()
    scatters[0].fill(product(s.x_t[...], s.grads[:, :h]))
    now[0].gather()
    now[2].relay()
    scatters[1].fill(product(s.cot_t[...], s.grads[:, h : 2 * h]))
    now[1].gather()
    now[0].relay()
    now[1].relay()
    scatters[0].start()
    scatters[1].start()
    for m in (2, 0, 1):
        now[m].finish(adjoint_put(m))
    for m in range(COUNT):
        s.current[m] = s.adjoint[m].astype(f32)
    ns_backward(s, 0, NS_STEPS - 1)
    scatters[0].forward()
    ns_backward(s, NS_STEPS - 1, NS_STEPS)
    s.b4[:, :f], s.b4[:, f : 2 * f], s.bow[:, :f] = ns_finish(s)

    def update_back(i, at):
        s.work[:, : 2 * f] = product(s.key[at, :], s.b4[:, : 2 * f])
        s.work[:, 2 * f :] = product(s.scaled[at, :], s.bow[:, :f])

        def point(j, col):
            here = pl.ds(j * sub, sub)
            to = rows_from(i, j)
            press_in = s.work[here, col : col + half]
            press_up = s.work[here, f + col : f + col + half]
            back_hid = s.work[here, 2 * f + col : 2 * f + col + half]
            pre_in, pre_up = s.pre[to, col : col + half], s.pre[to, f + col : f + col + half]
            up = s.ups[to, col : col + half]
            sigma, activation, slope = sigmoid_slope(pre_in)
            rest = 1.0 - sigma
            curvature = sigma * rest * (2.0 + pre_in * (rest - sigma))
            press_slope = press_in * slope
            s.hb[to, f + col : f + col + half] = rounded(press_slope * pre_up + press_up * activation)
            s.g4[to, 3 * f + col : 3 * f + col + half] = rounded(
                press_slope * up + back_hid * activation
            )
            s.g4[to, 2 * f + col : 2 * f + col + half] = rounded(
                press_in * up * pre_up * curvature + (press_up * up + back_hid * pre_up) * slope
            )

        over_subs(point)

    each_tile(update_back, 0, tiles // 2)
    scatters[1].forward()
    each_tile(update_back, tiles // 2, tiles)
    now = reduces[2]
    now[2].fill(product(s.scaled_t[...], s.hb[:, f:]))
    now[2].start()
    now[0].fill(product(s.key_t[...], s.g4[:, 2 * f : 3 * f]))
    now[0].start()
    now[1].fill(product(s.key_t[...], s.g4[:, 3 * f :]))
    now[1].start()

    def token_back(i, at):
        back_scaled = times_transpose(s.hb[at, :], s.bow[...])
        weighed = back_scaled * s.value[at, :].astype(f32)
        for t in range(tile // LANES):
            block = weighed[t * LANES : (t + 1) * LANES, :]
            folded = block[:, :LANES]
            for c in range(1, h // LANES):
                folded = folded + block[:, c * LANES : (c + 1) * LANES]
            s.rate_out[pl.ds(i * (tile // LANES) + t, 1), :] = jnp.sum(
                folded.T, axis=0, keepdims=True
            )
        s.grads[at, 2 * h :] = rounded(rate_of(at, h) * back_scaled)
        s.grads[at, h : 2 * h] = rounded(times_transpose(s.g4[at, :], s.b4[...]))

    over_tiles(token_back, 0, tiles // 2)
    now[2].forward()
    over_tiles(token_back, tiles // 2, tiles)
    stores = [
        load(s.rate_out, s.rate_hbm, s.store_sems.at[1]),
    ]
    now[0].forward()
    now[2].gather()
    key_value = product(s.x_t[...], s.grads[:, h:])
    scatters[2].fill(key_value)
    scatters[2].start()
    scatters[3].fill(key_value, h)
    scatters[3].start()
    now[1].forward()
    now[0].gather()

    def inputs_back(i, at):
        s.cot[at, :] = rounded(times_transpose(s.grads[at, :], s.wall[...]))

    now[2].relay()
    over_tiles(inputs_back)
    stores.append(load(s.cot, s.back_hbm, s.store_sems.at[0]))
    scatters[2].forward()
    now[1].gather()
    now[0].relay()
    scatters[3].forward()
    now[1].relay()

    def sum_put(m):
        def put(at, block):
            s.totals[m, at, :] = s.adjoint[m, at, :].astype(f32) + block

        return put

    for g, (to, sem) in enumerate(((s.query_hbm, 5), (s.output_hbm, 8))):
        s.row_sums[g] = scatters[g].total()
        stores.append(load(s.row_sums.at[g], to, s.store_sems.at[sem]))
    now[2].finish(sum_put(2))
    s.gout[...] = s.totals[2].T
    stores.append(load(s.gout, s.out_hbm, s.store_sems.at[4]))
    now[0].finish(sum_put(0))
    stores.append(load(s.totals.at[0], s.in_hbm, s.store_sems.at[2]))
    for g, (to, sem) in ((2, (s.key_hbm, 6)), (3, (s.value_hbm, 7))):
        s.row_sums[g] = scatters[g].total()
        stores.append(load(s.row_sums.at[g], to, s.store_sems.at[sem]))
    now[1].finish(sum_put(1))
    stores.append(load(s.totals.at[1], s.up_hbm, s.store_sems.at[3]))
    for copy in stores:
        copy.wait()


def pieces_of(shape, kind):
    size = math.prod(shape) * jnp.dtype(kind).itemsize
    count = max(1, min(size // PIECE, shape[0] // LANES))
    while shape[0] % (16 * count) and count > 1:
        count -= 1
    step = shape[0] // count
    return [pl.ds(i * step, step) for i in range(count)]


def copy_kernel(count, *refs):
    sources, targets, holds = (refs[i * count : (i + 1) * count] for i in range(3))
    sems = refs[-1]
    moves = [
        (src.at[at], hold.at[at], dst.at[at])
        for src, dst, hold in zip(sources, targets, holds)
        for at in pieces_of(src.shape, src.dtype)
    ]
    loads = [
        pltpu.make_async_copy(src, hold, sems.at[0, i])
        for i, (src, hold, _) in enumerate(moves)
    ]
    stores = [
        pltpu.make_async_copy(hold, dst, sems.at[1, i])
        for i, (_, hold, dst) in enumerate(moves)
    ]
    for load in loads:
        load.start()
    for load, store in zip(loads, stores):
        load.wait()
        store.start()
    for store in stores:
        store.wait()


def body(n, *operands):
    inputs, rates, fast_in = operands[0], operands[1], operands[6]
    tokens, width = inputs.shape
    h, f = fast_in.shape
    wide_rows = width // n
    bf16, f32 = jnp.bfloat16, jnp.float32
    outs = [
        ((tokens, width), bf16),
        ((tokens // LANES, LANES), f32),
        ((h, f), f32),
        ((h, f), f32),
        ((f, h), f32),
        ((wide_rows, h), f32),
        ((wide_rows, h), f32),
        ((wide_rows, h), f32),
        ((wide_rows, h), f32),
    ]
    scratch = scratch_of(n, tokens, width, h, f)
    anywhere = pl.BlockSpec(memory_space=pl.ANY)
    operands = list(operands)
    operands[1] = rates.reshape(tokens // LANES, LANES)
    results = pl.pallas_call(
        functools.partial(kernel, n, OPERANDS + RESULTS + tuple(scratch)),
        out_shape=[jax.ShapeDtypeStruct(shape, kind) for shape, kind in outs],
        in_specs=[anywhere] * len(operands),
        out_specs=[anywhere] * len(outs),
        scratch_shapes=list(scratch.values()),
        compiler_params=pltpu.CompilerParams(
            collective_id=0, has_side_effects=True, vmem_limit_bytes=VMEM_LIMIT
        ),
    )(*operands)

    moves = sum(len(pieces_of(shape, kind)) for shape, kind in outs)
    return pl.pallas_call(
        functools.partial(copy_kernel, len(outs)),
        out_shape=[jax.ShapeDtypeStruct(shape, kind) for shape, kind in outs],
        in_specs=[anywhere] * len(outs),
        out_specs=[anywhere] * len(outs),
        scratch_shapes=[pltpu.VMEM(shape, kind) for shape, kind in outs]
        + [pltpu.SemaphoreType.DMA((2, moves))],
    )(*results)


def solution(mesh):
    n = mesh.shape["seq"]

    def step(*operands):
        outs = body(n, *operands)
        return (outs[0], outs[1].reshape(-1)) + tuple(outs[2:8]) + (outs[8].T,)

    in_specs = (
        P(("batch", "seq"), None),
        P(("batch", "seq")),
        P(),
        P(),
        P(),
        P(),
        P(),
        P(),
        P(),
        P(("batch", "seq"), None),
    )
    out_specs = (
        P(("batch", "seq"), None),
        P(("batch", "seq")),
        P("batch", None),
        P("batch", None),
        P("batch", None),
        P("seq", "batch"),
        P("seq", "batch"),
        P("seq", "batch"),
        P("batch", "seq"),
    )
    return jax.shard_map(
        step, mesh=mesh, in_specs=in_specs, out_specs=out_specs, check_vma=False
    )
```
